512 devices in a mesh: chan: 8 (over z), space: 64 (over y, x, core).
Axes of the slice: x: 4, y: 8, z: 8, core: 2. Of those that a mesh axis runs over, the one named last changes fastest.
Arguments:
- cotangent: bfloat16 [80, 131072], P(None, 'space'), may hold values from -6 to 6
- pair_band: int32 [8192], P('space'), may hold values from 0 to 15
- pair_target: int32 [8192], P('space'), may hold values from 0 to 1023, as said below
- pair_count: int32 [64], P('space'), may hold values from 1 to 128, as said below
- pair_weight: bfloat16 [8192, 128, 128], P('space'), may hold values from -0.5 to 0.5
- head_weight: bfloat16 [512, 80], P('chan'), may hold values from -0.25 to 0.25
- features: bfloat16 [512, 131072], P('chan', 'space'), may hold values from -6 to 6
Outputs:
- feature_grad: bfloat16 [512, 131072], P('chan', 'space')
- weight_grad: float32 [512, 80], P('chan')
The draws below stay inside these ranges and needn't reach their ends.
Inputs may be any that keep to these rules, and one draw needn't show every extreme that they name: `pair_target`: targets of the slots of one device fall on each device's blocks (device index = target // 16) exactly 2 times, so at most 2 live pairs go from one device to one device; the first and last device of space have all slots live. `pair_count`: devices near both ends of space carry more live pairs than those in the middle.
All inputs are finite; a program needn't handle non-finite values.
Results may differ from the reference program's by a relative error of at most 0.0058.
Values may be sent and summed in bfloat16 or wider, within the bound.
No kernel may reach another device: no remote copies, remote signals or barrier semaphores. Data moves between devices by JAX's collectives and lax.ppermute only.
A program may use at most 64 MiB of HBM per device.

```python
import jax
import jax.numpy as jnp
from jax import lax

CH = 512
VARS = 80
B = 128
HPB = 16
LLB = 16
PMAX = 128
PAIRS = 8192
HP = 131072
LL = 131072
N_SPACE = 64


def draw_pair_target(key, part):

    def one_device(device_key):
        first_key, second_key = jax.random.split(device_key)
        dest_device = jax.random.permutation(first_key, jnp.arange(PMAX) % N_SPACE)
        local_block = jax.random.randint(second_key, (PMAX,), 0, HPB)
        return dest_device * HPB + local_block
    device_keys = jax.random.split(key, N_SPACE)
    return jax.vmap(one_device)(device_keys).reshape(PAIRS).astype(jnp.int32)


def draw_pair_count(key, part):
    device = jnp.arange(N_SPACE)
    distance = jnp.abs(2 * device - (N_SPACE - 1))
    baseline = N_SPACE // 4 + (PMAX - N_SPACE // 4) * distance * distance // (N_SPACE - 1) ** 2
    jitter = jax.random.randint(key, (N_SPACE,), 0, N_SPACE // 8 + 1)
    return jnp.minimum(baseline + jitter, PMAX).astype(jnp.int32)


def touch_ends(result, own_key, smallest, largest):
    longest = result.shape.index(max(result.shape))
    spots = []
    for shift in (0, 1):
        where = [jax.random.randint(jax.random.fold_in(own_key, axis), (), 0, length) for axis, length in enumerate(result.shape)]
        where[longest] = (where[longest] + shift) % result.shape[longest]
        spots.append(tuple(where))
    return result.at[spots[0]].set(smallest).at[spots[1]].set(largest)


def block_scale(rng, extent, pieces, least, largest):
    def one(position, shards_of):
        draws = jax.random.uniform(jax.random.fold_in(jax.random.fold_in(rng, 6), position), (shards_of,), jnp.float32, least / len(pieces), largest / len(pieces))
        return jnp.repeat(jnp.exp(draws), extent[position] // shards_of).reshape((-1,) + (1,) * (len(extent) - position - 1))

    loudness = one(*pieces[0])
    for cut in pieces[1:]:
        loudness = loudness * one(*cut)
    return loudness


def scatter_about(rng, dims, width, limit, pieces=(), kind=jnp.bfloat16):
    values = width * jax.random.normal(rng, dims, jnp.float32)
    if pieces:
        values = values * block_scale(rng, dims, pieces, -0.22, 0.18)
    return jnp.clip(values, -limit, limit).astype(kind)


def setup_inputs(seed: int = 0) -> dict:
    arg_keys = jax.random.split(jax.random.key(seed), 8)
    cotangent = scatter_about(arg_keys[0], (VARS, LL), 1.0, 6.0, ((1, 64),))
    pair_band = touch_ends(jax.random.randint(arg_keys[1], (PAIRS,), 0, LLB), jax.random.fold_in(arg_keys[1], 1), 0, LLB - 1).astype(jnp.int32)
    pair_target = draw_pair_target(jax.random.fold_in(arg_keys[7], 71), 0)
    pair_count = draw_pair_count(jax.random.fold_in(arg_keys[7], 71), 0)
    pair_weight = scatter_about(arg_keys[4], (PAIRS, B, B), B ** -0.5, 0.5, ((0, 64),))
    head_weight = scatter_about(arg_keys[5], (CH, VARS), CH ** -0.5, 0.25, ((0, 8),))
    features = scatter_about(arg_keys[6], (CH, HP), 1.0, 6.0, ((0, 8), (1, 64)))
    return {"cotangent": cotangent, "pair_band": pair_band, "pair_target": pair_target, "pair_count": pair_count, "pair_weight": pair_weight, "head_weight": head_weight, "features": features}


def reference(cotangent, pair_band, pair_target, pair_count, pair_weight, head_weight, features):
    band_blocks = cotangent.reshape(VARS, N_SPACE, LLB, B).transpose(1, 2, 0, 3)
    band_index = pair_band.reshape(N_SPACE, PMAX)
    targets = pair_target.reshape(N_SPACE, PMAX)
    weights = pair_weight.reshape(N_SPACE, PMAX, B, B)
    live_pair = jnp.arange(PMAX)[None, :] < pair_count[:, None]

    def one_device(running, device_items):
        blocks, index_row, target_row, weight_rows, live_row = device_items
        picked = blocks[index_row]
        contrib = jnp.einsum("pvr,prq->pvq", picked.astype(jnp.float32), weight_rows.astype(jnp.float32)).astype(jnp.bfloat16)
        contrib = jnp.where(live_row[:, None, None], contrib.astype(jnp.float32), jnp.float32(0.0))
        running = running + jax.ops.segment_sum(contrib, target_row, num_segments=N_SPACE * HPB)
        return running, None

    start = jnp.zeros((N_SPACE * HPB, VARS, B), jnp.float32)
    running, _ = lax.scan(one_device, start, (band_blocks, band_index, targets, weights, live_pair))
    pixel_grad = running.astype(jnp.bfloat16).transpose(1, 0, 2).reshape(VARS, HP)
    feature_grad = jnp.dot(head_weight, pixel_grad, preferred_element_type=jnp.float32).astype(jnp.bfloat16)
    weight_grad = jnp.dot(features, pixel_grad.T, preferred_element_type=jnp.float32) * (float(HP) ** -0.5)
    return feature_grad, weight_grad
```

```python
import functools

import jax
import jax.numpy as jnp
import numpy as np
from jax import lax
from jax.experimental import pallas as pl
from jax.experimental.pallas import tpu as pltpu
from jax.sharding import Mesh
from jax.sharding import PartitionSpec as P

NCHAN = 8
NSPACE = 64
VARS = 80
B = 128
SLOTS = 128
BLOCKS = 16
OWN = VARS // NCHAN
MSG = 24
CHUNK = 16
PART = OWN * BLOCKS
GROUP = 8
SPACE = ("y", "x", "core")
F32 = jnp.float32
BF16 = jnp.bfloat16


def contribute(band, target, count, place, cot, weight, out, lhs, acc, seen):
    step = pl.program_id(0)
    mine = place[0] // NSPACE
    space = place[0] % NSPACE

    @pl.when(step == 0)
    def _():
        for j in range(NSPACE):
            seen[j] = 0
        row = lax.broadcasted_iota(jnp.int32, (32, VARS), 0)
        col = lax.broadcasted_iota(jnp.int32, (32, VARS), 1)
        low = row & 15
        tail = low - 8 - 2 * (row >> 4)
        var = jnp.where(low < 8, low, jnp.where((tail >= 0) & (tail < 2), 8 + tail, -VARS * NCHAN))
        pick = jnp.where(col == var + mine * OWN, 1.0, 0.0).astype(BF16)
        rows = jnp.dot(pick, cot[...], preferred_element_type=F32).astype(BF16)
        for j in range(BLOCKS):
            for rank in range(2):
                lhs[2 * j + rank] = rows[16 * rank : 16 * rank + 16, j * B : (j + 1) * B]

    tag_row = lax.broadcasted_iota(jnp.int32, (8, B), 0)
    tag_lane = lax.broadcasted_iota(jnp.int32, (8, B), 1)
    tag_lane = jnp.where(tag_row == 4, tag_lane, -1)
    for i in range(CHUNK):
        slot = step * CHUNK + i
        dest = target[slot] >> 4
        rank = seen[dest]
        seen[dest] = rank + 1
        live = slot < count[0]
        value = jnp.dot(lhs[2 * band[slot] + rank], weight[i], preferred_element_type=F32)
        value = jnp.where(live, value, 0.0)
        tag = jnp.where(live, (target[slot] & 15) + 1, 0).astype(F32)
        extra = value[8:16] + jnp.where(tag_lane == 2 * space + rank, tag, 0.0)
        acc[dest, pl.ds(pl.multiple_of(8 * rank, 8), 8), :] = value[0:8]
        acc[dest, pl.ds(pl.multiple_of(16 + 8 * rank, 8), 8), :] = extra

    @pl.when(step == pl.num_programs(0) - 1)
    def _():
        def emit(k, carry):
            parts = []
            for half in range(2):
                x = acc[2 * k + half]
                parts += [x[0:16], x[16:24] + x[24:32]]
            rows = jnp.concatenate(parts, axis=0).astype(BF16)
            out[pl.ds(pl.multiple_of(2 * MSG * k, 2 * MSG), 2 * MSG), :] = rows
            return carry

        lax.fori_loop(0, NSPACE // 2, emit, 0, unroll=4)


def collect(got, tag_pick, spread, coef, out):
    x = got[...]
    tags = jnp.dot(tag_pick[...], x, preferred_element_type=F32).astype(BF16)
    label = jnp.dot(tags, spread[...], preferred_element_type=F32)[0:1]
    goal = jnp.where(label > 0.5, label * coef[0:1] + coef[1:2], -1.0)
    row = lax.broadcasted_iota(jnp.int32, (PART, NSPACE * MSG), 0).astype(F32)
    route = jnp.where(row == goal, 1.0, 0.0).astype(BF16)
    part = jnp.dot(route, x, preferred_element_type=F32).astype(BF16)
    for j in range(NCHAN):
        out[j] = part


def heads(parts, features, head, proj, fold, grad, share, wide):
    row = lax.broadcasted_iota(jnp.int32, (16, B), 0)
    main = [jnp.where((row >> 3) == k, 1.0, 0.0).astype(BF16) for k in range(2)]
    tail = [jnp.where((row >> 1) == k, 1.0, 0.0).astype(BF16) for k in range(8)]
    for b in range(BLOCKS):
        for c in range(NCHAN):
            base = PART * c + 32 + 16 * (b // 2)
            wide[16 * c : 16 * c + 16, b * B : (b + 1) * B] = parts[base : base + 16] * main[b % 2]
            base = PART * c + 16 * (b // 8)
            wide[128 + 16 * c : 144 + 16 * c, b * B : (b + 1) * B] = (
                parts[base : base + 16] * tail[b % 8]
            )
    k = wide[...]
    total = lax.dot_general(
        features[...], k, (((1,), (1,)), ((), ())), preferred_element_type=F32
    )
    total = jnp.dot(total, fold[...], preferred_element_type=F32, precision=lax.Precision.HIGHEST)
    for j in range(GROUP):
        share[j] = total
    lifted = jnp.dot(head[...], proj[...], preferred_element_type=F32).astype(BF16)
    grad[...] = jnp.dot(lifted, k, preferred_element_type=F32).astype(BF16)


def add_copies(got, out):
    total = got[0]
    for j in range(1, GROUP):
        total = total + got[j]
    for j in range(GROUP):
        out[j] = total


def add_last(scale, got, out):
    total = got[0]
    for j in range(1, GROUP):
        total = total + got[j]
    out[...] = (total * scale)[:, 0:VARS]


def tables():
    j = np.arange(NSPACE * MSG)
    src, t, r = j // MSG, (j % MSG) // 8, j % 8
    rank = np.where(t < 2, t, r // 2)
    data = (t < 2) | (r < 4)
    tag_pick = np.zeros((16, j.size), np.float32)
    tag_pick[0] = (t == 2) & (r == 4)
    spread = (np.arange(SLOTS)[:, None] == (2 * src + rank)[None]) & data[None]
    coef = np.zeros((8, j.size), np.float32)
    coef[0] = np.where(t < 2, 8, 2)
    coef[1] = np.where(t < 2, 32 - 8 + r, -2 + (r & 1))
    k = np.arange(256)
    c, i = (k % 128) // 16, k % 16
    var = OWN * c + np.where(k < 128, i % 8, 8 + i % 2)
    proj = np.arange(VARS)[:, None] == var[None]
    fold = var[:, None] == np.arange(B)[None]
    return (
        tag_pick.astype(BF16),
        spread.astype(BF16),
        coef,
        proj.astype(BF16),
        fold.astype(np.float32),
    )


def whole(shape):
    return jax.ShapeDtypeStruct(*shape)


def on_device(cotangent, pair_band, pair_target, pair_count, pair_weight, head_weight, features):
    tag_pick, spread, coef, proj, fold = tables()
    hp_local = features.shape[1]
    place = lax.axis_index(("chan",) + SPACE).astype(jnp.int32).reshape(1)
    sent = pl.pallas_call(
        contribute,
        out_shape=jax.ShapeDtypeStruct((NSPACE * MSG, B), BF16),
        grid_spec=pltpu.PrefetchScalarGridSpec(
            num_scalar_prefetch=4,
            grid=(SLOTS // CHUNK,),
            in_specs=[
                pl.BlockSpec((VARS, BLOCKS * B), lambda i, *_: (0, 0)),
                pl.BlockSpec((CHUNK, B, B), lambda i, *_: (i, 0, 0)),
            ],
            out_specs=pl.BlockSpec((NSPACE * MSG, B), lambda i, *_: (0, 0)),
            scratch_shapes=[
                pltpu.VMEM((2 * BLOCKS, 16, B), BF16),
                pltpu.VMEM((NSPACE, 32, B), F32),
                pltpu.SMEM((NSPACE,), jnp.int32),
            ],
        ),
        name="contribute",
    )(pair_band, pair_target, pair_count, place, cotangent, pair_weight)
    got = lax.all_to_all(sent.reshape(NSPACE, MSG, B), SPACE, 0, 0, tiled=True)
    parts = pl.pallas_call(
        collect,
        out_shape=jax.ShapeDtypeStruct((NCHAN, PART, B), BF16),
        name="collect",
    )(got.reshape(NSPACE * MSG, B), tag_pick, spread, coef)
    parts = lax.all_to_all(parts, "chan", 0, 0, tiled=True)
    feature_grad, share = pl.pallas_call(
        heads,
        out_shape=(
            jax.ShapeDtypeStruct((head_weight.shape[0], hp_local), BF16),
            jax.ShapeDtypeStruct((GROUP, head_weight.shape[0], B), F32),
        ),
        scratch_shapes=[pltpu.VMEM((256, hp_local), BF16)],
        name="heads",
    )(parts.reshape(NCHAN * PART, B), features, head_weight, proj, fold)
    share = lax.all_to_all(share, ("x", "core"), 0, 0, tiled=True)
    share = pl.pallas_call(
        add_copies, out_shape=jax.ShapeDtypeStruct(share.shape, F32), name="add_copies"
    )(share)
    share = lax.all_to_all(share, "y", 0, 0, tiled=True)
    grad_scale = float(hp_local * NSPACE) ** (-0.5)
    weight_grad = pl.pallas_call(
        functools.partial(add_last, grad_scale),
        out_shape=jax.ShapeDtypeStruct(head_weight.shape, F32),
        name="add_last",
    )(share)
    return feature_grad, weight_grad


def solution(mesh):
    fine = Mesh(mesh.devices.reshape(NCHAN, 8, 4, 2), ("chan",) + SPACE)
    placed = (
        P(None, SPACE),
        P(SPACE),
        P(SPACE),
        P(SPACE),
        P(SPACE, None, None),
        P("chan", None),
        P("chan", SPACE),
    )
    return jax.shard_map(
        on_device,
        mesh=fine,
        in_specs=placed,
        out_specs=(P("chan", SPACE), P("chan", None)),
        check_vma=False,
    )
```

```python
import functools

import jax
import jax.numpy as jnp
import numpy as np
from jax import lax
from jax.experimental import pallas as pl
from jax.experimental.pallas import tpu as pltpu
from jax.sharding import Mesh
from jax.sharding import PartitionSpec as P

NCHAN = 8
NSPACE = 64
VARS = 80
B = 128
SLOTS = 128
BLOCKS = 16
OWN = VARS // NCHAN
MSG = 24
CHUNK = 16
PART = OWN * BLOCKS
GROUP = 8
SPACE = ("y", "x", "core")
F32 = jnp.float32
BF16 = jnp.bfloat16


def contribute(
    place, count, band_in, target_in, cot_in, weight_in, out, band, target, cot, weight, lhs, acc, seen, sems,
):
    chunks = SLOTS // CHUNK
    small = [
        pltpu.make_async_copy(src, dst, sems.at[chunks + k])
        for k, (src, dst) in enumerate(
            ((cot_in, cot), (band_in, band), (target_in, target))
        )
    ]
    parts = [
        pltpu.make_async_copy(
            weight_in.at[pl.ds(k * CHUNK, CHUNK)], weight.at[pl.ds(k * CHUNK, CHUNK)], sems.at[k]
        )
        for k in range(chunks)
    ]
    for copy in small:
        copy.start()
    for copy in parts:
        copy.start()
    mine = place[0] // NSPACE
    space = place[0] % NSPACE
    for j in range(NSPACE):
        seen[j] = 0
    row = lax.broadcasted_iota(jnp.int32, (32, VARS), 0)
    col = lax.broadcasted_iota(jnp.int32, (32, VARS), 1)
    low = row & 15
    tail = low - 8 - 2 * (row >> 4)
    var = jnp.where(low < 8, low, jnp.where((tail >= 0) & (tail < 2), 8 + tail, -VARS * NCHAN))
    pick = jnp.where(col == var + mine * OWN, 1.0, 0.0).astype(BF16)
    tag_row = lax.broadcasted_iota(jnp.int32, (8, B), 0)
    tag_lane = lax.broadcasted_iota(jnp.int32, (8, B), 1)
    tag_lane = jnp.where(tag_row == 4, tag_lane, -1)
    small[0].wait()
    rows = jnp.dot(pick, cot[...], preferred_element_type=F32).astype(BF16)
    for j in range(BLOCKS):
        for rank in range(2):
            lhs[2 * j + rank] = rows[16 * rank : 16 * rank + 16, j * B : (j + 1) * B]
    for copy in small[1:]:
        copy.wait()

    def chunk(k, carry):
        base = k * CHUNK
        pltpu.make_async_copy(
            weight_in.at[pl.ds(base, CHUNK)], weight.at[pl.ds(base, CHUNK)], sems.at[k]
        ).wait()
        for i in range(CHUNK):
            slot = base + i
            dest = target[slot] >> 4
            rank = seen[dest]
            seen[dest] = rank + 1
            live = slot < count[0]
            value = jnp.dot(lhs[2 * band[slot] + rank], weight[slot], preferred_element_type=F32)
            value = jnp.where(live, value, 0.0)
            tag = jnp.where(live, (target[slot] & 15) + 1, 0).astype(F32)
            extra = value[8:16] + jnp.where(tag_lane == 2 * space + rank, tag, 0.0)
            acc[dest, pl.ds(pl.multiple_of(8 * rank, 8), 8), :] = value[0:8]
            acc[dest, pl.ds(pl.multiple_of(16 + 8 * rank, 8), 8), :] = extra
        return carry

    lax.fori_loop(0, chunks, chunk, 0)

    def emit(k, carry):
        parts = []
        for half in range(2):
            x = acc[2 * k + half]
            parts += [x[0:16], x[16:24] + x[24:32]]
        rows = jnp.concatenate(parts, axis=0).astype(BF16)
        out[pl.ds(pl.multiple_of(2 * MSG * k, 2 * MSG), 2 * MSG), :] = rows
        return carry

    lax.fori_loop(0, NSPACE // 2, emit, 0, unroll=4)


def collect(got, tag_pick, spread, coef, out):
    x = got[...]
    tags = jnp.dot(tag_pick[...], x, preferred_element_type=F32).astype(BF16)
    label = jnp.dot(tags, spread[...], preferred_element_type=F32)[0:1]
    goal = jnp.where(label > 0.5, label * coef[0:1] + coef[1:2], -1.0)
    row = lax.broadcasted_iota(jnp.int32, (PART, NSPACE * MSG), 0).astype(F32)
    route = jnp.where(row == goal, 1.0, 0.0).astype(BF16)
    part = jnp.dot(route, x, preferred_element_type=F32).astype(BF16)
    for j in range(NCHAN):
        out[j] = part


def widen(parts, wide):
    row = lax.broadcasted_iota(jnp.int32, (16, B), 0)
    main = [jnp.where((row >> 3) == k, 1.0, 0.0).astype(BF16) for k in range(2)]
    tail = [jnp.where((row >> 1) == k, 1.0, 0.0).astype(BF16) for k in range(8)]
    for b in range(BLOCKS):
        for c in range(NCHAN):
            base = PART * c + 32 + 16 * (b // 2)
            wide[16 * c : 16 * c + 16, b * B : (b + 1) * B] = parts[base : base + 16] * main[b % 2]
            base = PART * c + 16 * (b // 8)
            wide[128 + 16 * c : 144 + 16 * c, b * B : (b + 1) * B] = (
                parts[base : base + 16] * tail[b % 8]
            )


def weight_share(parts, features, fold, share, wide):
    widen(parts, wide)
    total = lax.dot_general(
        features[...], wide[...], (((1,), (1,)), ((), ())), preferred_element_type=F32
    )
    total = jnp.dot(total, fold[...], preferred_element_type=F32, precision=lax.Precision.HIGHEST)
    lane = lax.broadcasted_iota(jnp.int32, (64, B), 1)
    low = jnp.where(lane < 64, total, 0.0)
    high = jnp.where(lane < 64, 0.0, total)
    front = low[0:32] + pltpu.roll(low[32:64], 64, 1)
    back = high[32:40]
    for k in range(8):
        if k != 4:
            back = back + pltpu.roll(high[8 * k : 8 * k + 8], (16 * k - 64) % B, 1)
    for j in range(GROUP):
        share[j, 0:32] = front
        share[j, 32:40] = back


def feature_part(parts, head, proj, grad, wide):
    widen(parts, wide)
    lifted = jnp.dot(head[...], proj[...], preferred_element_type=F32).astype(BF16)
    grad[...] = jnp.dot(lifted, wide[...], preferred_element_type=F32).astype(BF16)


def add_up(got):
    total = got[0]
    for j in range(1, GROUP):
        total = total + got[j]
    return total


def add_copies(got, out):
    total = add_up(got)
    for j in range(GROUP):
        out[j] = total


def add_last(scale, got, out):
    total = add_up(got) * scale
    front, back = total[0:32], total[32:40]
    out[0:32, 0:64] = front[:, 0:64]
    out[32:64, 0:64] = pltpu.roll(front, 64, 1)[:, 0:64]
    for k in range(8):
        out[8 * k : 8 * k + 8, 64:VARS] = pltpu.roll(back, (64 - 16 * k) % B, 1)[:, 64:VARS]


def tables():
    j = np.arange(NSPACE * MSG)
    src, t, r = j // MSG, (j % MSG) // 8, j % 8
    rank = np.where(t < 2, t, r // 2)
    data = (t < 2) | (r < 4)
    tag_pick = np.zeros((16, j.size), np.float32)
    tag_pick[0] = (t == 2) & (r == 4)
    spread = (np.arange(SLOTS)[:, None] == (2 * src + rank)[None]) & data[None]
    coef = np.zeros((8, j.size), np.float32)
    coef[0] = np.where(t < 2, 8, 2)
    coef[1] = np.where(t < 2, 32 - 8 + r, -2 + (r & 1))
    k = np.arange(256)
    c, i = (k % 128) // 16, k % 16
    var = OWN * c + np.where(k < 128, i % 8, 8 + i % 2)
    proj = np.arange(VARS)[:, None] == var[None]
    fold = var[:, None] == np.arange(B)[None]
    return (
        tag_pick.astype(BF16),
        spread.astype(BF16),
        coef,
        proj.astype(BF16),
        fold.astype(np.float32),
    )


def small_grant(mib):
    return pltpu.CompilerParams(vmem_limit_bytes=mib << 20)


def near(x):
    return pltpu.with_memory_space_constraint(x, pltpu.VMEM)


def far(x):
    return pltpu.with_memory_space_constraint(x, pltpu.HBM)


def on_device(cotangent, pair_band, pair_target, pair_count, pair_weight, head_weight, features):
    tag_pick, spread, coef, proj, fold = tables()
    hp_local = features.shape[1]
    place = lax.axis_index(("chan",) + SPACE).astype(jnp.int32).reshape(1)
    hbm = pl.BlockSpec(memory_space=pltpu.HBM)
    sent = pl.pallas_call(
        contribute,
        out_shape=jax.ShapeDtypeStruct((NSPACE * MSG, B), BF16),
        in_specs=[pl.BlockSpec(memory_space=pltpu.SMEM)] * 2 + [hbm] * 4,
        scratch_shapes=[
            pltpu.SMEM((SLOTS,), jnp.int32),
            pltpu.SMEM((SLOTS,), jnp.int32),
            pltpu.VMEM((VARS, BLOCKS * B), BF16),
            pltpu.VMEM((SLOTS, B, B), BF16),
            pltpu.VMEM((2 * BLOCKS, 16, B), BF16),
            pltpu.VMEM((NSPACE, 32, B), F32),
            pltpu.SMEM((NSPACE,), jnp.int32),
            pltpu.SemaphoreType.DMA((SLOTS // CHUNK + 3,)),
        ],
        compiler_params=small_grant(12),
        name="contribute",
    )(place, pair_count, *map(far, (pair_band, pair_target, cotangent, pair_weight)))
    got = lax.all_to_all(sent.reshape(NSPACE, MSG, B), SPACE, 0, 0, tiled=True)
    parts = pl.pallas_call(
        collect,
        out_shape=jax.ShapeDtypeStruct((NCHAN, PART, B), BF16),
        compiler_params=small_grant(8),
        name="collect",
    )(near(got.reshape(NSPACE * MSG, B)), tag_pick, spread, coef)
    parts = lax.all_to_all(parts, "chan", 0, 0, tiled=True).reshape(NCHAN * PART, B)
    parts = near(parts)
    share = pl.pallas_call(
        weight_share,
        out_shape=jax.ShapeDtypeStruct((GROUP, 40, B), F32),
        scratch_shapes=[pltpu.VMEM((256, hp_local), BF16)],
        compiler_params=small_grant(8),
        name="weight_share",
    )(parts, features, fold)
    share = lax.all_to_all(share, ("x", "core"), 0, 0, tiled=True)
    feature_grad = pl.pallas_call(
        feature_part,
        out_shape=jax.ShapeDtypeStruct((head_weight.shape[0], hp_local), BF16),
        scratch_shapes=[pltpu.VMEM((256, hp_local), BF16)],
        compiler_params=small_grant(8),
        name="feature_part",
    )(parts, head_weight, proj)
    share = pl.pallas_call(
        add_copies,
        out_shape=jax.ShapeDtypeStruct(share.shape, F32),
        compiler_params=small_grant(2),
        name="add_copies",
    )(near(share))
    share = lax.all_to_all(share, "y", 0, 0, tiled=True)
    grad_scale = float(hp_local * NSPACE) ** (-0.5)
    weight_grad = pl.pallas_call(
        functools.partial(add_last, grad_scale),
        out_shape=jax.ShapeDtypeStruct(head_weight.shape, F32),
        compiler_params=small_grant(2),
        name="add_last",
    )(near(share))
    return feature_grad, weight_grad


def solution(mesh):
    fine = Mesh(mesh.devices.reshape(NCHAN, 8, 4, 2), ("chan",) + SPACE)
    placed = (
        P(None, SPACE),
        P(SPACE),
        P(SPACE),
        P(SPACE),
        P(SPACE, None, None),
        P("chan", None),
        P("chan", SPACE),
    )
    return jax.shard_map(
        on_device,
        mesh=fine,
        in_specs=placed,
        out_specs=(P("chan", SPACE), P("chan", None)),
        check_vma=False,
    )
```

```python
import functools

import jax
import jax.numpy as jnp
import numpy as np
from jax import lax
from jax.experimental import pallas as pl
from jax.experimental.pallas import tpu as pltpu
from jax.sharding import Mesh
from jax.sharding import PartitionSpec as P

NCHAN = 8
NSPACE = 64
VARS = 80
B = 128
SLOTS = 128
BLOCKS = 16
OWN = VARS // NCHAN
MSG = 24
CHUNK = 32
PART = OWN * BLOCKS
GROUP = 8
SPACE = ("y", "x", "core")
F32 = jnp.float32
BF16 = jnp.bfloat16


def contribute(
    place, count, band_in, target_in, cot_in, weight_in, out,
    band, target, cot, weight, lhs, acc, seen, sems,
):
    chunks = SLOTS // CHUNK
    small = [
        pltpu.make_async_copy(src, dst, sems.at[chunks + k])
        for k, (src, dst) in enumerate(
            ((cot_in, cot), (band_in, band), (target_in, target))
        )
    ]

    def part(k):
        at = pl.ds(pl.multiple_of(k * CHUNK, CHUNK), CHUNK)
        return pltpu.make_async_copy(weight_in.at[at], weight.at[at], sems.at[k])

    for copy in small:
        copy.start()
    for k in range(chunks):
        part(k).start()
    mine = place[0] // NSPACE
    space = place[0] % NSPACE
    for j in range(NSPACE):
        seen[j] = 2 * j
    row = lax.broadcasted_iota(jnp.int32, (32, VARS), 0)
    col = lax.broadcasted_iota(jnp.int32, (32, VARS), 1)
    low = row & 15
    tail = low - 8 - 2 * (row >> 4)
    var = jnp.where(low < 8, low, jnp.where((tail >= 0) & (tail < 2), 8 + tail, -VARS * NCHAN))
    pick = jnp.where(col == var + mine * OWN, 1.0, 0.0).astype(BF16)
    tag_row = lax.broadcasted_iota(jnp.int32, (8, B), 0)
    tag_lane = lax.broadcasted_iota(jnp.int32, (8, B), 1)
    tag_lane = jnp.where(tag_row == 4, tag_lane - 2 * space, -1)
    dead = 2 * BLOCKS
    lhs[dead] = jnp.zeros((16, B), BF16)
    small[0].wait()
    rows = jnp.dot(pick, cot[...], preferred_element_type=F32).astype(BF16)
    for j in range(BLOCKS):
        for rank in range(2):
            lhs[2 * j + rank] = rows[16 * rank : 16 * rank + 16, j * B : (j + 1) * B]
    for copy in small[1:]:
        copy.wait()
    live_slots = count[0]

    def chunk(k, carry):
        part(k).wait()
        for i in range(CHUNK):
            slot = k * CHUNK + i
            goal = target[slot]
            dest = goal >> 4
            key = seen[dest]
            seen[dest] = key + 1
            rank = key & 1
            live = slot < live_slots
            source = jnp.where(live, 2 * band[slot] + rank, dead)
            tag = jnp.where(live, (goal & 15) + 1, 0)
            value = jnp.dot(lhs[source], weight[slot], preferred_element_type=F32)
            acc[key, 0:8, :] = value[0:8]
            acc[key, 8:16, :] = value[8:16] + jnp.where(tag_lane == rank, tag, 0).astype(F32)
        return carry

    lax.fori_loop(0, chunks, chunk, 0)

    def emit(k, carry):
        parts = []
        for half in range(2):
            first, second = acc[4 * k + 2 * half], acc[4 * k + 2 * half + 1]
            parts += [first[0:8], second[0:8], first[8:16] + second[8:16]]
        rows = jnp.concatenate(parts, axis=0).astype(BF16)
        out[pl.ds(pl.multiple_of(2 * MSG * k, 2 * MSG), 2 * MSG), :] = rows
        return carry

    lax.fori_loop(0, NSPACE // 2, emit, 0, unroll=4)


def collect(got, tag_pick, spread, coef, out):
    x = got[...]
    tags = jnp.dot(tag_pick[...], x, preferred_element_type=F32).astype(BF16)
    label = jnp.dot(tags, spread[...], preferred_element_type=F32)[0:1]
    goal = jnp.where(label > 0.5, label * coef[0:1] + coef[1:2], -1.0)
    row = lax.broadcasted_iota(jnp.int32, (PART, NSPACE * MSG), 0).astype(F32)
    route = jnp.where(row == goal, 1.0, 0.0).astype(BF16)
    part = jnp.dot(route, x, preferred_element_type=F32).astype(BF16)
    for j in range(NCHAN):
        out[j] = part


def widen(parts, wide):
    row = lax.broadcasted_iota(jnp.int32, (16, B), 0)
    main = [jnp.where((row >> 3) == k, 1.0, 0.0).astype(BF16) for k in range(2)]
    tail = [jnp.where((row >> 1) == k, 1.0, 0.0).astype(BF16) for k in range(8)]
    for b in range(BLOCKS):
        for c in range(NCHAN):
            base = PART * c + 32 + 16 * (b // 2)
            wide[16 * c : 16 * c + 16, b * B : (b + 1) * B] = parts[base : base + 16] * main[b % 2]
            base = PART * c + 16 * (b // 8)
            wide[128 + 16 * c : 144 + 16 * c, b * B : (b + 1) * B] = (
                parts[base : base + 16] * tail[b % 8]
            )


def weight_share(parts, features, fold, share, wide):
    widen(parts, wide)
    total = lax.dot_general(
        features[...], wide[...], (((1,), (1,)), ((), ())), preferred_element_type=F32
    )
    total = jnp.dot(total, fold[...], preferred_element_type=F32, precision=lax.Precision.HIGHEST)
    lane = lax.broadcasted_iota(jnp.int32, (64, B), 1)
    low = jnp.where(lane < 64, total, 0.0)
    high = jnp.where(lane < 64, 0.0, total)
    front = low[0:32] + pltpu.roll(low[32:64], 64, 1)
    back = high[32:40]
    for k in range(8):
        if k != 4:
            back = back + pltpu.roll(high[8 * k : 8 * k + 8], (16 * k - 64) % B, 1)
    for j in range(GROUP):
        share[j, 0:32] = front
        share[j, 32:40] = back


def feature_part(parts, head, proj, grad, wide):
    widen(parts, wide)
    lifted = jnp.dot(head[...], proj[...], preferred_element_type=F32).astype(BF16)
    grad[...] = jnp.dot(lifted, wide[...], preferred_element_type=F32).astype(BF16)


def add_up(got):
    total = got[0]
    for j in range(1, GROUP):
        total = total + got[j]
    return total


def add_copies(got, out):
    total = add_up(got)
    for j in range(GROUP):
        out[j] = total


def add_last(scale, got, out):
    total = add_up(got) * scale
    front, back = total[0:32], total[32:40]
    out[0:32, 0:64] = front[:, 0:64]
    out[32:64, 0:64] = pltpu.roll(front, 64, 1)[:, 0:64]
    for k in range(8):
        out[8 * k : 8 * k + 8, 64:VARS] = pltpu.roll(back, (64 - 16 * k) % B, 1)[:, 64:VARS]


def tables():
    j = np.arange(NSPACE * MSG)
    src, t, r = j // MSG, (j % MSG) // 8, j % 8
    rank = np.where(t < 2, t, r // 2)
    data = (t < 2) | (r < 4)
    tag_pick = np.zeros((16, j.size), np.float32)
    tag_pick[0] = (t == 2) & (r == 4)
    spread = (np.arange(SLOTS)[:, None] == (2 * src + rank)[None]) & data[None]
    coef = np.zeros((8, j.size), np.float32)
    coef[0] = np.where(t < 2, 8, 2)
    coef[1] = np.where(t < 2, 32 - 8 + r, -2 + (r & 1))
    k = np.arange(256)
    c, i = (k % 128) // 16, k % 16
    var = OWN * c + np.where(k < 128, i % 8, 8 + i % 2)
    proj = np.arange(VARS)[:, None] == var[None]
    fold = var[:, None] == np.arange(B)[None]
    return (
        tag_pick.astype(BF16),
        spread.astype(BF16),
        coef,
        proj.astype(BF16),
        fold.astype(np.float32),
    )


def small_grant(mib):
    return pltpu.CompilerParams(vmem_limit_bytes=mib << 20)


def near(x):
    return pltpu.with_memory_space_constraint(x, pltpu.VMEM)


def far(x):
    return pltpu.with_memory_space_constraint(x, pltpu.HBM)


def on_device(cotangent, pair_band, pair_target, pair_count, pair_weight, head_weight, features):
    tag_pick, spread, coef, proj, fold = tables()
    hp_local = features.shape[1]
    place = lax.axis_index(("chan",) + SPACE).astype(jnp.int32).reshape(1)
    hbm = pl.BlockSpec(memory_space=pltpu.HBM)
    sent = pl.pallas_call(
        contribute,
        out_shape=jax.ShapeDtypeStruct((NSPACE * MSG, B), BF16),
        in_specs=[pl.BlockSpec(memory_space=pltpu.SMEM)] * 2 + [hbm] * 4,
        scratch_shapes=[
            pltpu.SMEM((SLOTS,), jnp.int32),
            pltpu.SMEM((SLOTS,), jnp.int32),
            pltpu.VMEM((VARS, BLOCKS * B), BF16),
            pltpu.VMEM((SLOTS, B, B), BF16),
            pltpu.VMEM((2 * BLOCKS + 1, 16, B), BF16),
            pltpu.VMEM((SLOTS, 16, B), F32),
            pltpu.SMEM((NSPACE,), jnp.int32),
            pltpu.SemaphoreType.DMA((SLOTS // CHUNK + 3,)),
        ],
        compiler_params=small_grant(12),
        name="contribute",
    )(place, pair_count, *map(far, (pair_band, pair_target, cotangent, pair_weight)))
    got = lax.all_to_all(sent.reshape(NSPACE, MSG, B), SPACE, 0, 0, tiled=True)
    parts = pl.pallas_call(
        collect,
        out_shape=jax.ShapeDtypeStruct((NCHAN, PART, B), BF16),
        compiler_params=small_grant(8),
        name="collect",
    )(near(got.reshape(NSPACE * MSG, B)), tag_pick, spread, coef)
    parts = lax.all_to_all(parts, "chan", 0, 0, tiled=True).reshape(NCHAN * PART, B)
    parts = near(parts)
    share = pl.pallas_call(
        weight_share,
        out_shape=jax.ShapeDtypeStruct((GROUP, 40, B), F32),
        scratch_shapes=[pltpu.VMEM((256, hp_local), BF16)],
        compiler_params=small_grant(8),
        name="weight_share",
    )(parts, features, fold)
    share = lax.all_to_all(share, ("x", "core"), 0, 0, tiled=True)
    feature_grad = pl.pallas_call(
        feature_part,
        out_shape=jax.ShapeDtypeStruct((head_weight.shape[0], hp_local), BF16),
        scratch_shapes=[pltpu.VMEM((256, hp_local), BF16)],
        compiler_params=small_grant(8),
        name="feature_part",
    )(parts, head_weight, proj)
    share = pl.pallas_call(
        add_copies,
        out_shape=jax.ShapeDtypeStruct(share.shape, F32),
        compiler_params=small_grant(2),
        name="add_copies",
    )(near(share))
    share = lax.all_to_all(share, "y", 0, 0, tiled=True)
    grad_scale = float(hp_local * NSPACE) ** (-0.5)
    weight_grad = pl.pallas_call(
        functools.partial(add_last, grad_scale),
        out_shape=jax.ShapeDtypeStruct(head_weight.shape, F32),
        compiler_params=small_grant(2),
        name="add_last",
    )(near(share))
    return feature_grad, weight_grad


def solution(mesh):
    fine = Mesh(mesh.devices.reshape(NCHAN, 8, 4, 2), ("chan",) + SPACE)
    placed = (
        P(None, SPACE),
        P(SPACE),
        P(SPACE),
        P(SPACE),
        P(SPACE, None, None),
        P("chan", None),
        P("chan", SPACE),
    )
    return jax.shard_map(
        on_device,
        mesh=fine,
        in_specs=placed,
        out_specs=(P("chan", SPACE), P("chan", None)),
        check_vma=False,
    )
```

```python
import functools

import jax
import jax.numpy as jnp
import numpy as np
from jax import lax
from jax.experimental import pallas as pl
from jax.experimental.pallas import tpu as pltpu
from jax.sharding import Mesh
from jax.sharding import PartitionSpec as P

NCHAN = 8
NSPACE = 64
VARS = 80
B = 128
SLOTS = 128
BLOCKS = 16
OWN = VARS // NCHAN
MSG = 24
CHUNK = 32
PART = OWN * BLOCKS
GROUP = 8
SPACE = ("y", "x", "core")
F32 = jnp.float32
BF16 = jnp.bfloat16


def contribute(
    place, count, band_in, target_in, cot_in, weight_in, out,
    band, target, cot, weight, lhs, acc, seen, sems,
):
    chunks = SLOTS // CHUNK
    small = [
        pltpu.make_async_copy(src, dst, sems.at[chunks + k])
        for k, (src, dst) in enumerate(
            ((cot_in, cot), (band_in, band), (target_in, target))
        )
    ]

    def part(k):
        at = pl.ds(pl.multiple_of(k * CHUNK, CHUNK), CHUNK)
        return pltpu.make_async_copy(weight_in.at[at], weight.at[at], sems.at[k])

    for copy in small:
        copy.start()
    live_slots = count[0]
    groups = (live_slots + (CHUNK - 1)) // CHUNK
    for k in range(chunks):

        @pl.when(k < groups)
        def _():
            part(k).start()

    mine = place[0] // NSPACE
    space = place[0] % NSPACE
    for j in range(NSPACE):
        seen[j] = 2 * j
    row = lax.broadcasted_iota(jnp.int32, (32, VARS), 0)
    col = lax.broadcasted_iota(jnp.int32, (32, VARS), 1)
    low = row & 15
    tail = low - 8 - 2 * (row >> 4)
    var = jnp.where(low < 8, low, jnp.where((tail >= 0) & (tail < 2), 8 + tail, -VARS * NCHAN))
    pick = jnp.where(col == var + mine * OWN, 1.0, 0.0).astype(BF16)
    tag_row = lax.broadcasted_iota(jnp.int32, (8, B), 0)
    tag_lane = lax.broadcasted_iota(jnp.int32, (8, B), 1)
    tag_lane = jnp.where(tag_row == 4, tag_lane - 2 * space, -1)
    dead = 2 * BLOCKS
    lhs[dead] = jnp.zeros((16, B), BF16)
    acc[...] = jnp.zeros_like(acc)
    small[0].wait()
    rows = jnp.dot(pick, cot[...], preferred_element_type=F32).astype(BF16)
    for j in range(BLOCKS):
        for rank in range(2):
            lhs[2 * j + rank] = rows[16 * rank : 16 * rank + 16, j * B : (j + 1) * B]
    for copy in small[1:]:
        copy.wait()

    def chunk(k, carry):
        part(k).wait()
        for i in range(CHUNK):
            slot = k * CHUNK + i
            goal = target[slot]
            dest = goal >> 4
            key = seen[dest]
            seen[dest] = key + 1
            rank = key & 1
            live = slot < live_slots
            source = jnp.where(live, 2 * band[slot] + rank, dead)
            tag = jnp.where(live, (goal & 15) + 1, 0)
            value = jnp.dot(lhs[source], weight[slot], preferred_element_type=F32)
            acc[key, 0:8, :] = value[0:8]
            acc[key, 8:16, :] = value[8:16] + jnp.where(tag_lane == rank, tag, 0).astype(F32)
        return carry

    lax.fori_loop(0, groups, chunk, 0)

    def emit(k, carry):
        parts = []
        for half in range(2):
            first, second = acc[4 * k + 2 * half], acc[4 * k + 2 * half + 1]
            parts += [first[0:8], second[0:8], first[8:16] + second[8:16]]
        rows = jnp.concatenate(parts, axis=0).astype(BF16)
        out[pl.ds(pl.multiple_of(2 * MSG * k, 2 * MSG), 2 * MSG), :] = rows
        return carry

    lax.fori_loop(0, NSPACE // 2, emit, 0, unroll=4)


def collect(got, tag_pick, spread, coef, out):
    x = got[...]
    tags = jnp.dot(tag_pick[...], x, preferred_element_type=F32).astype(BF16)
    label = jnp.dot(tags, spread[...], preferred_element_type=F32)[0:1]
    goal = jnp.where(label > 0.5, label * coef[0:1] + coef[1:2], -1.0)
    row = lax.broadcasted_iota(jnp.int32, (PART, NSPACE * MSG), 0).astype(F32)
    route = jnp.where(row == goal, 1.0, 0.0).astype(BF16)
    part = jnp.dot(route, x, preferred_element_type=F32).astype(BF16)
    for j in range(NCHAN):
        out[j] = part


def widen(parts, wide):
    row = lax.broadcasted_iota(jnp.int32, (16, B), 0)
    main = [jnp.where((row >> 3) == k, 1.0, 0.0).astype(BF16) for k in range(2)]
    tail = [jnp.where((row >> 1) == k, 1.0, 0.0).astype(BF16) for k in range(8)]
    for b in range(BLOCKS):
        for c in range(NCHAN):
            base = PART * c + 32 + 16 * (b // 2)
            wide[16 * c : 16 * c + 16, b * B : (b + 1) * B] = parts[base : base + 16] * main[b % 2]
            base = PART * c + 16 * (b // 8)
            wide[128 + 16 * c : 144 + 16 * c, b * B : (b + 1) * B] = (
                parts[base : base + 16] * tail[b % 8]
            )


def weight_share(parts, features, fold, share, wide):
    widen(parts, wide)
    total = lax.dot_general(
        features[...], wide[...], (((1,), (1,)), ((), ())), preferred_element_type=F32
    )
    total = jnp.dot(total, fold[...], preferred_element_type=F32, precision=lax.Precision.HIGHEST)
    lane = lax.broadcasted_iota(jnp.int32, (64, B), 1)
    low = jnp.where(lane < 64, total, 0.0)
    high = jnp.where(lane < 64, 0.0, total)
    front = low[0:32] + pltpu.roll(low[32:64], 64, 1)
    back = high[32:40]
    for k in range(8):
        if k != 4:
            back = back + pltpu.roll(high[8 * k : 8 * k + 8], (16 * k - 64) % B, 1)
    for j in range(GROUP):
        share[j, 0:32] = front
        share[j, 32:40] = back


def feature_part(parts, head, proj, grad, wide):
    widen(parts, wide)
    lifted = jnp.dot(head[...], proj[...], preferred_element_type=F32).astype(BF16)
    grad[...] = jnp.dot(lifted, wide[...], preferred_element_type=F32).astype(BF16)


def add_up(got):
    total = got[0]
    for j in range(1, GROUP):
        total = total + got[j]
    return total


def add_copies(got, out):
    total = add_up(got)
    for j in range(GROUP):
        out[j] = total


def add_last(scale, got, out):
    total = add_up(got) * scale
    front, back = total[0:32], total[32:40]
    out[0:32, 0:64] = front[:, 0:64]
    out[32:64, 0:64] = pltpu.roll(front, 64, 1)[:, 0:64]
    for k in range(8):
        out[8 * k : 8 * k + 8, 64:VARS] = pltpu.roll(back, (64 - 16 * k) % B, 1)[:, 64:VARS]


def tables():
    j = np.arange(NSPACE * MSG)
    src, t, r = j // MSG, (j % MSG) // 8, j % 8
    rank = np.where(t < 2, t, r // 2)
    data = (t < 2) | (r < 4)
    tag_pick = np.zeros((16, j.size), np.float32)
    tag_pick[0] = (t == 2) & (r == 4)
    spread = (np.arange(SLOTS)[:, None] == (2 * src + rank)[None]) & data[None]
    coef = np.zeros((8, j.size), np.float32)
    coef[0] = np.where(t < 2, 8, 2)
    coef[1] = np.where(t < 2, 32 - 8 + r, -2 + (r & 1))
    k = np.arange(256)
    c, i = (k % 128) // 16, k % 16
    var = OWN * c + np.where(k < 128, i % 8, 8 + i % 2)
    proj = np.arange(VARS)[:, None] == var[None]
    fold = var[:, None] == np.arange(B)[None]
    return (
        tag_pick.astype(BF16),
        spread.astype(BF16),
        coef,
        proj.astype(BF16),
        fold.astype(np.float32),
    )


def small_grant(mib):
    return pltpu.CompilerParams(vmem_limit_bytes=mib << 20)


def near(x):
    return pltpu.with_memory_space_constraint(x, pltpu.VMEM)


def far(x):
    return pltpu.with_memory_space_constraint(x, pltpu.HBM)


def on_device(cotangent, pair_band, pair_target, pair_count, pair_weight, head_weight, features):
    tag_pick, spread, coef, proj, fold = tables()
    hp_local = features.shape[1]
    place = lax.axis_index(("chan",) + SPACE).astype(jnp.int32).reshape(1)
    hbm = pl.BlockSpec(memory_space=pltpu.HBM)
    sent = pl.pallas_call(
        contribute,
        out_shape=jax.ShapeDtypeStruct((NSPACE * MSG, B), BF16),
        in_specs=[pl.BlockSpec(memory_space=pltpu.SMEM)] * 2 + [hbm] * 4,
        scratch_shapes=[
            pltpu.SMEM((SLOTS,), jnp.int32),
            pltpu.SMEM((SLOTS,), jnp.int32),
            pltpu.VMEM((VARS, BLOCKS * B), BF16),
            pltpu.VMEM((SLOTS, B, B), BF16),
            pltpu.VMEM((2 * BLOCKS + 1, 16, B), BF16),
            pltpu.VMEM((SLOTS, 16, B), F32),
            pltpu.SMEM((NSPACE,), jnp.int32),
            pltpu.SemaphoreType.DMA((SLOTS // CHUNK + 3,)),
        ],
        compiler_params=small_grant(12),
        name="contribute",
    )(place, pair_count, *map(far, (pair_band, pair_target, cotangent, pair_weight)))
    got = lax.all_to_all(sent.reshape(NSPACE, MSG, B), SPACE, 0, 0, tiled=True)
    parts = pl.pallas_call(
        collect,
        out_shape=jax.ShapeDtypeStruct((NCHAN, PART, B), BF16),
        compiler_params=small_grant(8),
        name="collect",
    )(near(got.reshape(NSPACE * MSG, B)), tag_pick, spread, coef)
    parts = lax.all_to_all(parts, "chan", 0, 0, tiled=True).reshape(NCHAN * PART, B)
    parts = near(parts)
    share = pl.pallas_call(
        weight_share,
        out_shape=jax.ShapeDtypeStruct((GROUP, 40, B), F32),
        scratch_shapes=[pltpu.VMEM((256, hp_local), BF16)],
        compiler_params=small_grant(8),
        name="weight_share",
    )(parts, features, fold)
    share = lax.all_to_all(share, ("x", "core"), 0, 0, tiled=True)
    feature_grad = pl.pallas_call(
        feature_part,
        out_shape=jax.ShapeDtypeStruct((head_weight.shape[0], hp_local), BF16),
        scratch_shapes=[pltpu.VMEM((256, hp_local), BF16)],
        compiler_params=small_grant(8),
        name="feature_part",
    )(parts, head_weight, proj)
    share = pl.pallas_call(
        add_copies,
        out_shape=jax.ShapeDtypeStruct(share.shape, F32),
        compiler_params=small_grant(2),
        name="add_copies",
    )(near(share))
    share = lax.all_to_all(share, "y", 0, 0, tiled=True)
    grad_scale = float(hp_local * NSPACE) ** (-0.5)
    weight_grad = pl.pallas_call(
        functools.partial(add_last, grad_scale),
        out_shape=jax.ShapeDtypeStruct(head_weight.shape, F32),
        compiler_params=small_grant(2),
        name="add_last",
    )(near(share))
    return feature_grad, weight_grad


def solution(mesh):
    fine = Mesh(mesh.devices.reshape(NCHAN, 8, 4, 2), ("chan",) + SPACE)
    placed = (
        P(None, SPACE),
        P(SPACE),
        P(SPACE),
        P(SPACE),
        P(SPACE, None, None),
        P("chan", None),
        P("chan", SPACE),
    )
    return jax.shard_map(
        on_device,
        mesh=fine,
        in_specs=placed,
        out_specs=(P("chan", SPACE), P("chan", None)),
        check_vma=False,
    )
```

```python
import functools

import jax
import jax.numpy as jnp
import numpy as np
from jax import lax
from jax.experimental import pallas as pl
from jax.experimental.pallas import tpu as pltpu
from jax.sharding import Mesh
from jax.sharding import PartitionSpec as P

NCHAN = 8
NSPACE = 64
VARS = 80
B = 128
SLOTS = 128
BLOCKS = 16
OWN = VARS // NCHAN
MSG = 24
CHUNK = 32
PART = OWN * BLOCKS
GROUP = 8
SPACE = ("y", "x", "core")
F32 = jnp.float32
BF16 = jnp.bfloat16


def contribute(
    place, count, band_in, target_in, cot_in, weight_in, out,
    band, target, cot, weight, lhs, acc, seen, sems,
):
    chunks = SLOTS // CHUNK
    small = [
        pltpu.make_async_copy(src, dst, sems.at[chunks + k])
        for k, (src, dst) in enumerate(
            ((cot_in, cot), (band_in, band), (target_in, target))
        )
    ]

    def part(k):
        at = pl.ds(pl.multiple_of(k * CHUNK, CHUNK), CHUNK)
        return pltpu.make_async_copy(weight_in.at[at], weight.at[at], sems.at[k])

    for copy in small:
        copy.start()
    live_slots = count[0]
    groups = (live_slots + (CHUNK - 1)) // CHUNK
    for k in range(chunks):

        @pl.when(k < groups)
        def _():
            part(k).start()

    mine = place[0] // NSPACE
    space = place[0] % NSPACE
    for j in range(NSPACE):
        seen[j] = 2 * j
    row = lax.broadcasted_iota(jnp.int32, (32, VARS), 0)
    col = lax.broadcasted_iota(jnp.int32, (32, VARS), 1)
    low = row & 15
    tail = low - 8 - 2 * (row >> 4)
    var = jnp.where(low < 8, low, jnp.where((tail >= 0) & (tail < 2), 8 + tail, -VARS * NCHAN))
    pick = jnp.where(col == var + mine * OWN, 1.0, 0.0).astype(BF16)
    tag_row = lax.broadcasted_iota(jnp.int32, (8, B), 0)
    tag_lane = lax.broadcasted_iota(jnp.int32, (8, B), 1)
    tag_lane = jnp.where(tag_row == 4, tag_lane - 2 * space, -1)
    dead = 2 * BLOCKS
    lhs[dead] = jnp.zeros((16, B), BF16)
    acc[...] = jnp.zeros_like(acc)
    small[0].wait()
    rows = jnp.dot(pick, cot[...], preferred_element_type=F32).astype(BF16)
    for j in range(BLOCKS):
        for rank in range(2):
            lhs[2 * j + rank] = rows[16 * rank : 16 * rank + 16, j * B : (j + 1) * B]
    for copy in small[1:]:
        copy.wait()

    def chunk(k, carry):
        part(k).wait()
        for i in range(CHUNK):
            slot = k * CHUNK + i
            goal = target[slot]
            dest = goal >> 4
            key = seen[dest]
            seen[dest] = key + 1
            rank = key & 1
            live = slot < live_slots
            source = jnp.where(live, 2 * band[slot] + rank, dead)
            tag = jnp.where(live, (goal & 15) + 1, 0)
            value = jnp.dot(lhs[source], weight[slot], preferred_element_type=F32)
            acc[key, 0:8, :] = value[0:8]
            acc[key, 8:16, :] = value[8:16] + jnp.where(tag_lane == rank, tag, 0).astype(F32)
        return carry

    lax.fori_loop(0, groups, chunk, 0)

    def emit(k, carry):
        parts = []
        for half in range(2):
            first, second = acc[4 * k + 2 * half], acc[4 * k + 2 * half + 1]
            parts += [first[0:8], second[0:8], first[8:16] + second[8:16]]
        rows = jnp.concatenate(parts, axis=0).astype(BF16)
        out[pl.ds(pl.multiple_of(2 * MSG * k, 2 * MSG), 2 * MSG), :] = rows
        return carry

    lax.fori_loop(0, NSPACE // 2, emit, 0, unroll=4)


def collect(got, tag_pick, spread, coef, out):
    x = got[...]
    tags = jnp.dot(tag_pick[...], x, preferred_element_type=F32).astype(BF16)
    label = jnp.dot(tags, spread[...], preferred_element_type=F32)[0:1]
    goal = jnp.where(label > 0.5, label * coef[0:1] + coef[1:2], -1.0)
    row = lax.broadcasted_iota(jnp.int32, (PART, NSPACE * MSG), 0).astype(F32)
    route = jnp.where(row == goal, 1.0, 0.0).astype(BF16)
    part = jnp.dot(route, x, preferred_element_type=F32).astype(BF16)
    for j in range(NCHAN):
        out[j] = part


def widen(parts, wide):
    row = lax.broadcasted_iota(jnp.int32, (16, B), 0)
    main = [jnp.where((row >> 3) == k, 1.0, 0.0).astype(BF16) for k in range(2)]
    tail = [jnp.where((row >> 1) == k, 1.0, 0.0).astype(BF16) for k in range(8)]
    for b in range(BLOCKS):
        for c in range(NCHAN):
            base = PART * c + 32 + 16 * (b // 2)
            wide[16 * c : 16 * c + 16, b * B : (b + 1) * B] = parts[base : base + 16] * main[b % 2]
            base = PART * c + 16 * (b // 8)
            wide[128 + 16 * c : 144 + 16 * c, b * B : (b + 1) * B] = (
                parts[base : base + 16] * tail[b % 8]
            )


def heads(parts, features, head, proj, fold, grad_out, share, wide, grad, sem):
    widen(parts, wide)
    lifted = jnp.dot(head[...], proj[...], preferred_element_type=F32).astype(BF16)
    grad[...] = jnp.dot(lifted, wide[...], preferred_element_type=F32).astype(BF16)
    copy = pltpu.make_async_copy(grad, grad_out, sem)
    copy.start()
    total = lax.dot_general(
        features[...], wide[...], (((1,), (1,)), ((), ())), preferred_element_type=F32
    )
    total = jnp.dot(total, fold[...], preferred_element_type=F32, precision=lax.Precision.HIGHEST)
    lane = lax.broadcasted_iota(jnp.int32, (64, B), 1)
    low = jnp.where(lane < 64, total, 0.0)
    high = jnp.where(lane < 64, 0.0, total)
    front = low[0:32] + pltpu.roll(low[32:64], 64, 1)
    back = high[32:40]
    for k in range(8):
        if k != 4:
            back = back + pltpu.roll(high[8 * k : 8 * k + 8], (16 * k - 64) % B, 1)
    for j in range(GROUP):
        share[j, 0:32] = front
        share[j, 32:40] = back
    copy.wait()


def add_up(got):
    total = got[0]
    for j in range(1, GROUP):
        total = total + got[j]
    return total


def add_copies(got, out):
    total = add_up(got)
    for j in range(GROUP):
        out[j] = total


def add_last(scale, got, out):
    total = add_up(got) * scale
    front, back = total[0:32], total[32:40]
    out[0:32, 0:64] = front[:, 0:64]
    out[32:64, 0:64] = pltpu.roll(front, 64, 1)[:, 0:64]
    for k in range(8):
        out[8 * k : 8 * k + 8, 64:VARS] = pltpu.roll(back, (64 - 16 * k) % B, 1)[:, 64:VARS]


def tables():
    j = np.arange(NSPACE * MSG)
    src, t, r = j // MSG, (j % MSG) // 8, j % 8
    rank = np.where(t < 2, t, r // 2)
    data = (t < 2) | (r < 4)
    tag_pick = np.zeros((16, j.size), np.float32)
    tag_pick[0] = (t == 2) & (r == 4)
    spread = (np.arange(SLOTS)[:, None] == (2 * src + rank)[None]) & data[None]
    coef = np.zeros((8, j.size), np.float32)
    coef[0] = np.where(t < 2, 8, 2)
    coef[1] = np.where(t < 2, 32 - 8 + r, -2 + (r & 1))
    k = np.arange(256)
    c, i = (k % 128) // 16, k % 16
    var = OWN * c + np.where(k < 128, i % 8, 8 + i % 2)
    proj = np.arange(VARS)[:, None] == var[None]
    fold = var[:, None] == np.arange(B)[None]
    return (
        tag_pick.astype(BF16),
        spread.astype(BF16),
        coef,
        proj.astype(BF16),
        fold.astype(np.float32),
    )


def small_grant(mib):
    return pltpu.CompilerParams(vmem_limit_bytes=mib << 20)


def near(x):
    return pltpu.with_memory_space_constraint(x, pltpu.VMEM)


def far(x):
    return pltpu.with_memory_space_constraint(x, pltpu.HBM)


def on_device(cotangent, pair_band, pair_target, pair_count, pair_weight, head_weight, features):
    tag_pick, spread, coef, proj, fold = tables()
    hp_local = features.shape[1]
    place = lax.axis_index(("chan",) + SPACE).astype(jnp.int32).reshape(1)
    hbm = pl.BlockSpec(memory_space=pltpu.HBM)
    sent = pl.pallas_call(
        contribute,
        out_shape=jax.ShapeDtypeStruct((NSPACE * MSG, B), BF16),
        in_specs=[pl.BlockSpec(memory_space=pltpu.SMEM)] * 2 + [hbm] * 4,
        scratch_shapes=[
            pltpu.SMEM((SLOTS,), jnp.int32),
            pltpu.SMEM((SLOTS,), jnp.int32),
            pltpu.VMEM((VARS, BLOCKS * B), BF16),
            pltpu.VMEM((SLOTS, B, B), BF16),
            pltpu.VMEM((2 * BLOCKS + 1, 16, B), BF16),
            pltpu.VMEM((SLOTS, 16, B), F32),
            pltpu.SMEM((NSPACE,), jnp.int32),
            pltpu.SemaphoreType.DMA((SLOTS // CHUNK + 3,)),
        ],
        compiler_params=small_grant(12),
        name="contribute",
    )(place, pair_count, *map(far, (pair_band, pair_target, cotangent, pair_weight)))
    got = lax.all_to_all(sent.reshape(NSPACE, MSG, B), SPACE, 0, 0, tiled=True)
    parts = pl.pallas_call(
        collect,
        out_shape=jax.ShapeDtypeStruct((NCHAN, PART, B), BF16),
        compiler_params=small_grant(8),
        name="collect",
    )(near(got.reshape(NSPACE * MSG, B)), tag_pick, spread, coef)
    parts = lax.all_to_all(parts, "chan", 0, 0, tiled=True).reshape(NCHAN * PART, B)
    parts = near(parts)
    feature_grad, share = pl.pallas_call(
        heads,
        out_shape=(
            jax.ShapeDtypeStruct((head_weight.shape[0], hp_local), BF16),
            jax.ShapeDtypeStruct((GROUP, 40, B), F32),
        ),
        out_specs=(hbm, pl.BlockSpec(memory_space=pltpu.VMEM)),
        scratch_shapes=[
            pltpu.VMEM((256, hp_local), BF16),
            pltpu.VMEM((head_weight.shape[0], hp_local), BF16),
            pltpu.SemaphoreType.DMA(()),
        ],
        compiler_params=small_grant(8),
        name="heads",
    )(parts, features, head_weight, proj, fold)
    share = lax.all_to_all(share, ("x", "core"), 0, 0, tiled=True)
    share = pl.pallas_call(
        add_copies,
        out_shape=jax.ShapeDtypeStruct(share.shape, F32),
        compiler_params=small_grant(2),
        name="add_copies",
    )(near(share))
    share = lax.all_to_all(share, "y", 0, 0, tiled=True)
    grad_scale = float(hp_local * NSPACE) ** (-0.5)
    weight_grad = pl.pallas_call(
        functools.partial(add_last, grad_scale),
        out_shape=jax.ShapeDtypeStruct(head_weight.shape, F32),
        compiler_params=small_grant(2),
        name="add_last",
    )(near(share))
    return feature_grad, weight_grad


def solution(mesh):
    fine = Mesh(mesh.devices.reshape(NCHAN, 8, 4, 2), ("chan",) + SPACE)
    placed = (
        P(None, SPACE),
        P(SPACE),
        P(SPACE),
        P(SPACE),
        P(SPACE, None, None),
        P("chan", None),
        P("chan", SPACE),
    )
    return jax.shard_map(
        on_device,
        mesh=fine,
        in_specs=placed,
        out_specs=(P("chan", SPACE), P("chan", None)),
        check_vma=False,
    )
```

```python
import functools

import jax
import jax.numpy as jnp
import numpy as np
from jax import lax
from jax.experimental import pallas as pl
from jax.experimental.pallas import tpu as pltpu
from jax.sharding import Mesh
from jax.sharding import PartitionSpec as P

NCHAN = 8
NSPACE = 64
VARS = 80
B = 128
SLOTS = 128
BLOCKS = 16
OWN = VARS // NCHAN
MSG = 22
CHUNK = 32
PART = OWN * BLOCKS
GROUP = 8
SPACE = ("y", "x", "core")
F32 = jnp.float32
BF16 = jnp.bfloat16


def contribute(
    place, count, band_in, target_in, cot_in, weight_in, out,
    band, target, cot, weight, lhs, acc, seen, sems,
):
    chunks = SLOTS // CHUNK
    small = [
        pltpu.make_async_copy(src, dst, sems.at[chunks + k])
        for k, (src, dst) in enumerate(
            ((cot_in, cot), (band_in, band), (target_in, target))
        )
    ]

    def part(k):
        at = pl.ds(pl.multiple_of(k * CHUNK, CHUNK), CHUNK)
        return pltpu.make_async_copy(weight_in.at[at], weight.at[at], sems.at[k])

    for copy in small:
        copy.start()
    live_slots = count[0]
    groups = (live_slots + (CHUNK - 1)) // CHUNK
    for k in range(chunks):

        @pl.when(k < groups)
        def _():
            part(k).start()

    mine = place[0] // NSPACE
    space = place[0] % NSPACE
    for j in range(NSPACE):
        seen[j] = 2 * j
    row = lax.broadcasted_iota(jnp.int32, (32, VARS), 0)
    col = lax.broadcasted_iota(jnp.int32, (32, VARS), 1)
    low = row & 15
    tail = low - 8 - 2 * (row >> 4)
    var = jnp.where(low < 8, low, jnp.where((tail >= 0) & (tail < 2), 8 + tail, -VARS * NCHAN))
    pick = jnp.where(col == var + mine * OWN, 1.0, 0.0).astype(BF16)
    tag_row = lax.broadcasted_iota(jnp.int32, (8, B), 0)
    tag_lane = lax.broadcasted_iota(jnp.int32, (8, B), 1)
    tag_lane = jnp.where(tag_row == 4, tag_lane - 2 * space, -1)
    dead = 2 * BLOCKS
    lhs[dead] = jnp.zeros((16, B), BF16)
    acc[...] = jnp.zeros_like(acc)
    small[0].wait()
    rows = jnp.dot(pick, cot[...], preferred_element_type=F32).astype(BF16)
    for j in range(BLOCKS):
        for rank in range(2):
            lhs[2 * j + rank] = rows[16 * rank : 16 * rank + 16, j * B : (j + 1) * B]
    for copy in small[1:]:
        copy.wait()

    def chunk(k, carry):
        part(k).wait()
        for i in range(CHUNK):
            slot = k * CHUNK + i
            goal = target[slot]
            dest = goal >> 4
            key = seen[dest]
            seen[dest] = key + 1
            rank = key & 1
            live = slot < live_slots
            source = jnp.where(live, 2 * band[slot] + rank, dead)
            tag = jnp.where(live, (goal & 15) + 1, 0)
            value = jnp.dot(lhs[source], weight[slot], preferred_element_type=F32)
            acc[key, 0:8, :] = value[0:8]
            acc[key, 8:16, :] = value[8:16] + jnp.where(tag_lane == rank, tag, 0).astype(F32)
        return carry

    lax.fori_loop(0, groups, chunk, 0)

    sub = lax.broadcasted_iota(jnp.int32, (8, B), 0)

    def emit(k, carry):
        tiles = []
        for quad in range(2):
            first, second, extra, turned = [], [], [], []
            for h in range(4):
                one, two = acc[16 * k + 8 * quad + 2 * h], acc[16 * k + 8 * quad + 2 * h + 1]
                first.append(one[0:8])
                second.append(two[0:8])
                extra.append(one[8:16] + two[8:16])
                turned.append(pltpu.roll(extra[h], 2, 0))
            for h in range(4):
                tiles += [first[h], second[h]]
                if h < 3:
                    tiles.append(jnp.where(sub < 6 - 2 * h, extra[h], turned[h + 1]))
        rows = jnp.concatenate(tiles, axis=0).astype(BF16)
        out[pl.ds(pl.multiple_of(8 * MSG * k, 8 * MSG), 8 * MSG), :] = rows
        return carry

    lax.fori_loop(0, NSPACE // 8, emit, 0)


def collect(place, got, col, out):
    x = got[...]
    columns = NSPACE * MSG
    turn = (2 * (place[0] & 3)).astype(F32)
    at = col[0:1] - turn
    at = jnp.where(at < 0, at + MSG, at)
    src = col[1:2]
    main = at < 15.5
    rank = jnp.where(main, jnp.where(at < 7.5, 0.0, 1.0), jnp.where(at < 17.5, 0.0, 1.0))
    slot = jnp.where(at < 19.5, 2 * src + rank, -1.0)
    row = lax.broadcasted_iota(jnp.int32, (PART, columns), 0).astype(F32)
    spread = jnp.where(row[0:SLOTS] == slot, 1.0, 0.0).astype(BF16)
    tag_row = jnp.where(jnp.abs(at - 20) < 0.5, 0.0, -1.0)
    tag_pick = jnp.where(row[0:16] == tag_row, 1.0, 0.0).astype(BF16)
    tags = jnp.dot(tag_pick, x, preferred_element_type=F32).astype(BF16)
    label = jnp.dot(tags, spread, preferred_element_type=F32)[0:1]
    goal = jnp.where(main, 8 * label + (24 + at - 8 * rank), 2 * label + (at - 18 - 2 * rank))
    goal = jnp.where(label > 0.5, goal, -1.0)
    route = jnp.where(row == goal, 1.0, 0.0).astype(BF16)
    part = jnp.dot(route, x, preferred_element_type=F32).astype(BF16)
    for j in range(NCHAN):
        out[j] = part


def widen(parts, wide):
    row = lax.broadcasted_iota(jnp.int32, (16, B), 0)
    main = [jnp.where((row >> 3) == k, 1.0, 0.0).astype(BF16) for k in range(2)]
    tail = [jnp.where((row >> 1) == k, 1.0, 0.0).astype(BF16) for k in range(8)]
    for b in range(BLOCKS):
        for c in range(NCHAN):
            base = PART * c + 32 + 16 * (b // 2)
            wide[16 * c : 16 * c + 16, b * B : (b + 1) * B] = parts[base : base + 16] * main[b % 2]
            base = PART * c + 16 * (b // 8)
            wide[128 + 16 * c : 144 + 16 * c, b * B : (b + 1) * B] = (
                parts[base : base + 16] * tail[b % 8]
            )


def heads(parts, features, head, proj, fold, grad_out, share, wide, grad, sem):
    widen(parts, wide)
    lifted = jnp.dot(head[...], proj[...], preferred_element_type=F32).astype(BF16)
    grad[...] = jnp.dot(lifted, wide[...], preferred_element_type=F32).astype(BF16)
    copy = pltpu.make_async_copy(grad, grad_out, sem)
    copy.start()
    total = lax.dot_general(
        features[...], wide[...], (((1,), (1,)), ((), ())), preferred_element_type=F32
    )
    total = jnp.dot(total, fold[...], preferred_element_type=F32, precision=lax.Precision.HIGHEST)
    lane = lax.broadcasted_iota(jnp.int32, (64, B), 1)
    low = jnp.where(lane < 64, total, 0.0)
    high = jnp.where(lane < 64, 0.0, total)
    front = low[0:32] + pltpu.roll(low[32:64], 64, 1)
    back = high[32:40]
    for k in range(8):
        if k != 4:
            back = back + pltpu.roll(high[8 * k : 8 * k + 8], (16 * k - 64) % B, 1)
    for j in range(GROUP):
        share[j, 0:32] = front
        share[j, 32:40] = back
    copy.wait()


def add_up(got):
    total = got[0]
    for j in range(1, GROUP):
        total = total + got[j]
    return total


def add_copies(got, out):
    total = add_up(got)
    for j in range(GROUP):
        out[j] = total


def add_last(scale, got, out):
    total = add_up(got) * scale
    front, back = total[0:32], total[32:40]
    out[0:32, 0:64] = front[:, 0:64]
    out[32:64, 0:64] = pltpu.roll(front, 64, 1)[:, 0:64]
    for k in range(8):
        out[8 * k : 8 * k + 8, 64:VARS] = pltpu.roll(back, (64 - 16 * k) % B, 1)[:, 64:VARS]


def tables():
    j = np.arange(NSPACE * MSG)
    col = np.zeros((8, j.size), np.float32)
    col[0] = j % MSG
    col[1] = j // MSG
    k = np.arange(256)
    c, i = (k % 128) // 16, k % 16
    var = OWN * c + np.where(k < 128, i % 8, 8 + i % 2)
    proj = np.arange(VARS)[:, None] == var[None]
    fold = var[:, None] == np.arange(B)[None]
    return col, proj.astype(BF16), fold.astype(np.float32)


def small_grant(mib):
    return pltpu.CompilerParams(vmem_limit_bytes=mib << 20)


def near(x):
    return pltpu.with_memory_space_constraint(x, pltpu.VMEM)


def far(x):
    return pltpu.with_memory_space_constraint(x, pltpu.HBM)


def on_device(cotangent, pair_band, pair_target, pair_count, pair_weight, head_weight, features):
    col, proj, fold = tables()
    hp_local = features.shape[1]
    place = lax.axis_index(("chan",) + SPACE).astype(jnp.int32).reshape(1)
    hbm = pl.BlockSpec(memory_space=pltpu.HBM)
    sent = pl.pallas_call(
        contribute,
        out_shape=jax.ShapeDtypeStruct((NSPACE * MSG, B), BF16),
        in_specs=[pl.BlockSpec(memory_space=pltpu.SMEM)] * 2 + [hbm] * 4,
        scratch_shapes=[
            pltpu.SMEM((SLOTS,), jnp.int32),
            pltpu.SMEM((SLOTS,), jnp.int32),
            pltpu.VMEM((VARS, BLOCKS * B), BF16),
            pltpu.VMEM((SLOTS, B, B), BF16),
            pltpu.VMEM((2 * BLOCKS + 1, 16, B), BF16),
            pltpu.VMEM((SLOTS, 16, B), F32),
            pltpu.SMEM((NSPACE,), jnp.int32),
            pltpu.SemaphoreType.DMA((SLOTS // CHUNK + 3,)),
        ],
        compiler_params=small_grant(12),
        name="contribute",
    )(place, pair_count, *map(far, (pair_band, pair_target, cotangent, pair_weight)))
    got = lax.all_to_all(sent.reshape(NSPACE, MSG // 2, 2, B), SPACE, 0, 0, tiled=True)
    parts = pl.pallas_call(
        collect,
        out_shape=jax.ShapeDtypeStruct((NCHAN, PART, B), BF16),
        in_specs=[pl.BlockSpec(memory_space=pltpu.SMEM)]
        + [pl.BlockSpec(memory_space=pltpu.VMEM)] * 2,
        compiler_params=small_grant(8),
        name="collect",
    )(place, near(got.reshape(NSPACE * MSG, B)), col)
    parts = lax.all_to_all(parts, "chan", 0, 0, tiled=True).reshape(NCHAN * PART, B)
    parts = near(parts)
    feature_grad, share = pl.pallas_call(
        heads,
        out_shape=(
            jax.ShapeDtypeStruct((head_weight.shape[0], hp_local), BF16),
            jax.ShapeDtypeStruct((GROUP, 40, B), F32),
        ),
        out_specs=(hbm, pl.BlockSpec(memory_space=pltpu.VMEM)),
        scratch_shapes=[
            pltpu.VMEM((256, hp_local), BF16),
            pltpu.VMEM((head_weight.shape[0], hp_local), BF16),
            pltpu.SemaphoreType.DMA(()),
        ],
        compiler_params=small_grant(8),
        name="heads",
    )(parts, features, head_weight, proj, fold)
    share = lax.all_to_all(share, ("x", "core"), 0, 0, tiled=True)
    share = pl.pallas_call(
        add_copies,
        out_shape=jax.ShapeDtypeStruct(share.shape, F32),
        compiler_params=small_grant(2),
        name="add_copies",
    )(near(share))
    share = lax.all_to_all(share, "y", 0, 0, tiled=True)
    grad_scale = float(hp_local * NSPACE) ** (-0.5)
    weight_grad = pl.pallas_call(
        functools.partial(add_last, grad_scale),
        out_shape=jax.ShapeDtypeStruct(head_weight.shape, F32),
        compiler_params=small_grant(2),
        name="add_last",
    )(near(share))
    return feature_grad, weight_grad


def solution(mesh):
    fine = Mesh(mesh.devices.reshape(NCHAN, 8, 4, 2), ("chan",) + SPACE)
    placed = (
        P(None, SPACE),
        P(SPACE),
        P(SPACE),
        P(SPACE),
        P(SPACE, None, None),
        P("chan", None),
        P("chan", SPACE),
    )
    return jax.shard_map(
        on_device,
        mesh=fine,
        in_specs=placed,
        out_specs=(P("chan", SPACE), P("chan", None)),
        check_vma=False,
    )
```

```python
import functools

import jax
import jax.numpy as jnp
import numpy as np
from jax import lax
from jax.experimental import pallas as pl
from jax.experimental.pallas import tpu as pltpu
from jax.sharding import Mesh
from jax.sharding import PartitionSpec as P

NCHAN = 8
NSPACE = 64
VARS = 80
B = 128
SLOTS = 128
BLOCKS = 16
OWN = VARS // NCHAN
MSG = 22
CHUNK = 32
PART = OWN * BLOCKS
GROUP = 8
SPACE = ("y", "x", "core")
F32 = jnp.float32
BF16 = jnp.bfloat16


def contribute(
    place, count, band_in, target_in, cot_in, weight_in, out,
    band, target, cot, weight, lhs, acc, seen, sems,
):
    chunks = SLOTS // CHUNK
    small = [
        pltpu.make_async_copy(src, dst, sems.at[chunks + k])
        for k, (src, dst) in enumerate(
            ((cot_in, cot), (band_in, band), (target_in, target))
        )
    ]

    def part(k):
        at = pl.ds(pl.multiple_of(k * CHUNK, CHUNK), CHUNK)
        return pltpu.make_async_copy(weight_in.at[at], weight.at[at], sems.at[k])

    for copy in small:
        copy.start()
    live_slots = count[0]
    groups = (live_slots + (CHUNK - 1)) // CHUNK
    for k in range(chunks):

        @pl.when(k < groups)
        def _():
            part(k).start()

    mine = place[0] // NSPACE
    space = place[0] % NSPACE
    for j in range(NSPACE):
        seen[j] = 2 * j
    row = lax.broadcasted_iota(jnp.int32, (32, VARS), 0)
    col = lax.broadcasted_iota(jnp.int32, (32, VARS), 1)
    low = row & 15
    tail = low - 8 - 2 * (row >> 4)
    var = jnp.where(low < 8, low, jnp.where((tail >= 0) & (tail < 2), 8 + tail, -VARS * NCHAN))
    pick = jnp.where(col == var + mine * OWN, 1.0, 0.0).astype(BF16)
    tag_row = lax.broadcasted_iota(jnp.int32, (8, B), 0)
    tag_lane = lax.broadcasted_iota(jnp.int32, (8, B), 1)
    tag_lane = jnp.where(tag_row == 4, tag_lane - 2 * space, -1)
    dead = 2 * BLOCKS
    lhs[dead] = jnp.zeros((16, B), BF16)
    acc[...] = jnp.zeros_like(acc)
    small[0].wait()
    rows = jnp.dot(pick, cot[...], preferred_element_type=F32).astype(BF16)
    for j in range(BLOCKS):
        for rank in range(2):
            lhs[2 * j + rank] = rows[16 * rank : 16 * rank + 16, j * B : (j + 1) * B]
    for copy in small[1:]:
        copy.wait()

    def chunk(k, carry):
        part(k).wait()
        for i in range(CHUNK):
            slot = k * CHUNK + i
            goal = target[slot]
            dest = goal >> 4
            key = seen[dest]
            seen[dest] = key + 1
            rank = key & 1
            live = slot < live_slots
            source = jnp.where(live, 2 * band[slot] + rank, dead)
            tag = jnp.where(live, (goal & 15) + 1, 0)
            value = jnp.dot(lhs[source], weight[slot], preferred_element_type=F32)
            acc[key, 0:8, :] = value[0:8]
            acc[key, 8:16, :] = value[8:16] + jnp.where(tag_lane == rank, tag, 0).astype(F32)
        return carry

    lax.fori_loop(0, groups, chunk, 0)

    sub = lax.broadcasted_iota(jnp.int32, (8, B), 0)

    def emit(k, carry):
        tiles = []
        for quad in range(2):
            first, second, extra, turned = [], [], [], []
            for h in range(4):
                one, two = acc[16 * k + 8 * quad + 2 * h], acc[16 * k + 8 * quad + 2 * h + 1]
                first.append(one[0:8])
                second.append(two[0:8])
                extra.append(one[8:16] + two[8:16])
                turned.append(pltpu.roll(extra[h], 2, 0))
            for h in range(4):
                tiles += [first[h], second[h]]
                if h < 3:
                    tiles.append(jnp.where(sub < 6 - 2 * h, extra[h], turned[h + 1]))
        rows = jnp.concatenate(tiles, axis=0).astype(BF16)
        out[pl.ds(pl.multiple_of(8 * MSG * k, 8 * MSG), 8 * MSG), :] = rows
        return carry

    lax.fori_loop(0, NSPACE // 8, emit, 0)


def collect(place, got, col, out):
    x = got[...]
    columns = NSPACE * MSG
    turn = (2 * (place[0] & 3)).astype(F32)
    at = col[0:1] - turn
    at = jnp.where(at < 0, at + MSG, at)
    src = col[1:2]
    main = at < 15.5
    rank = jnp.where(main, jnp.where(at < 7.5, 0.0, 1.0), jnp.where(at < 17.5, 0.0, 1.0))
    slot = jnp.where(at < 19.5, 2 * src + rank, -1.0)
    row = lax.broadcasted_iota(jnp.int32, (PART, columns), 0).astype(F32)
    spread = jnp.where(row[0:SLOTS] == slot, 1.0, 0.0).astype(BF16)
    tag_row = jnp.where(jnp.abs(at - 20) < 0.5, 0.0, -1.0)
    tag_pick = jnp.where(row[0:16] == tag_row, 1.0, 0.0).astype(BF16)
    tags = jnp.dot(tag_pick, x, preferred_element_type=F32).astype(BF16)
    label = jnp.dot(tags, spread, preferred_element_type=F32)[0:1]
    goal = jnp.where(main, 8 * label + (24 + at - 8 * rank), 2 * label + (at - 18 - 2 * rank))
    goal = jnp.where(label > 0.5, goal, -1.0)
    route = jnp.where(row == goal, 1.0, 0.0).astype(BF16)
    part = jnp.dot(route, x, preferred_element_type=F32).astype(BF16)
    for j in range(NCHAN):
        out[j] = part


def heads(parts, features, head, proj, fold, grad_out, share, grad, sem):
    def gather(at):
        return jnp.concatenate(
            [parts[PART * c + at : PART * c + at + 16] for c in range(NCHAN)], axis=0
        )

    tails = [gather(16 * k) for k in range(2)]
    mains = [gather(32 + 16 * k) for k in range(8)]
    lane = lax.broadcasted_iota(jnp.int32, (64, B), 1) & 15
    lifted = jnp.dot(head[...], proj[...], preferred_element_type=F32)
    low = [jnp.where((lane >> 3) == k, lifted[:, 0:B], 0.0).astype(BF16) for k in range(2)]
    high = [jnp.where((lane >> 1) == k, lifted[:, B:], 0.0).astype(BF16) for k in range(8)]
    for pair in range(BLOCKS // 2):
        left = jnp.concatenate(
            [
                jnp.concatenate([low[k], high[(2 * pair + k) % 8]], axis=1)
                for k in range(2)
            ],
            axis=0,
        )
        right = jnp.concatenate([mains[pair], tails[pair // 4]], axis=0)
        both = jnp.dot(left, right, preferred_element_type=F32).astype(BF16)
        for k in range(2):
            grad[:, (2 * pair + k) * B : (2 * pair + k + 1) * B] = both[64 * k : 64 * k + 64]
    copy = pltpu.make_async_copy(grad, grad_out, sem)
    copy.start()

    def block(b):
        return features[:, b * B : (b + 1) * B]

    def product(left, right):
        return lax.dot_general(left, right, (((1,), (1,)), ((), ())), preferred_element_type=F32)

    paired = [
        jnp.concatenate([block(2 * k + half) for k in range(8)], axis=1) for half in range(2)
    ]
    total_main = product(jnp.concatenate(paired, axis=0), jnp.concatenate(mains, axis=1))
    eight = [jnp.concatenate([block(k), block(8 + k)], axis=1) for k in range(8)]
    total_tail = product(jnp.concatenate(eight, axis=0), jnp.concatenate(tails, axis=1))
    main = jnp.where((lane >> 3) == 0, total_main[0:64], total_main[64:128])
    tail = total_tail[0:64]
    for k in range(1, 8):
        tail = jnp.where((lane >> 1) == k, total_tail[64 * k : 64 * k + 64], tail)
    total = jnp.dot(
        jnp.concatenate([main, tail], axis=1),
        fold[...],
        preferred_element_type=F32,
        precision=lax.Precision.HIGHEST,
    )
    full = lax.broadcasted_iota(jnp.int32, (64, B), 1)
    first = jnp.where(full < 64, total, 0.0)
    rest = jnp.where(full < 64, 0.0, total)
    front = first[0:32] + pltpu.roll(first[32:64], 64, 1)
    back = rest[32:40]
    for k in range(8):
        if k != 4:
            back = back + pltpu.roll(rest[8 * k : 8 * k + 8], (16 * k - 64) % B, 1)
    for j in range(GROUP):
        share[j, 0:32] = front
        share[j, 32:40] = back
    copy.wait()


def add_up(got):
    total = got[0]
    for j in range(1, GROUP):
        total = total + got[j]
    return total


def add_copies(got, out):
    total = add_up(got)
    for j in range(GROUP):
        out[j] = total


def add_last(scale, got, out):
    total = add_up(got) * scale
    front, back = total[0:32], total[32:40]
    out[0:32, 0:64] = front[:, 0:64]
    out[32:64, 0:64] = pltpu.roll(front, 64, 1)[:, 0:64]
    for k in range(8):
        out[8 * k : 8 * k + 8, 64:VARS] = pltpu.roll(back, (64 - 16 * k) % B, 1)[:, 64:VARS]


def tables():
    j = np.arange(NSPACE * MSG)
    col = np.zeros((8, j.size), np.float32)
    col[0] = j % MSG
    col[1] = j // MSG
    k = np.arange(256)
    c, i = (k % 128) // 16, k % 16
    var = OWN * c + np.where(k < 128, i % 8, 8 + i % 2)
    proj = np.arange(VARS)[:, None] == var[None]
    fold = var[:, None] == np.arange(B)[None]
    return col, proj.astype(BF16), fold.astype(np.float32)


def small_grant(mib):
    return pltpu.CompilerParams(vmem_limit_bytes=mib << 20)


def near(x):
    return pltpu.with_memory_space_constraint(x, pltpu.VMEM)


def far(x):
    return pltpu.with_memory_space_constraint(x, pltpu.HBM)


def on_device(cotangent, pair_band, pair_target, pair_count, pair_weight, head_weight, features):
    col, proj, fold = tables()
    hp_local = features.shape[1]
    place = lax.axis_index(("chan",) + SPACE).astype(jnp.int32).reshape(1)
    hbm = pl.BlockSpec(memory_space=pltpu.HBM)
    sent = pl.pallas_call(
        contribute,
        out_shape=jax.ShapeDtypeStruct((NSPACE * MSG, B), BF16),
        in_specs=[pl.BlockSpec(memory_space=pltpu.SMEM)] * 2 + [hbm] * 4,
        scratch_shapes=[
            pltpu.SMEM((SLOTS,), jnp.int32),
            pltpu.SMEM((SLOTS,), jnp.int32),
            pltpu.VMEM((VARS, BLOCKS * B), BF16),
            pltpu.VMEM((SLOTS, B, B), BF16),
            pltpu.VMEM((2 * BLOCKS + 1, 16, B), BF16),
            pltpu.VMEM((SLOTS, 16, B), F32),
            pltpu.SMEM((NSPACE,), jnp.int32),
            pltpu.SemaphoreType.DMA((SLOTS // CHUNK + 3,)),
        ],
        compiler_params=small_grant(12),
        name="contribute",
    )(place, pair_count, *map(far, (pair_band, pair_target, cotangent, pair_weight)))
    got = lax.all_to_all(sent.reshape(NSPACE, MSG // 2, 2, B), SPACE, 0, 0, tiled=True)
    parts = pl.pallas_call(
        collect,
        out_shape=jax.ShapeDtypeStruct((NCHAN, PART, B), BF16),
        in_specs=[pl.BlockSpec(memory_space=pltpu.SMEM)]
        + [pl.BlockSpec(memory_space=pltpu.VMEM)] * 2,
        compiler_params=small_grant(8),
        name="collect",
    )(place, near(got.reshape(NSPACE * MSG, B)), col)
    parts = lax.all_to_all(parts, "chan", 0, 0, tiled=True).reshape(NCHAN * PART, B)
    parts = near(parts)
    feature_grad, share = pl.pallas_call(
        heads,
        out_shape=(
            jax.ShapeDtypeStruct((head_weight.shape[0], hp_local), BF16),
            jax.ShapeDtypeStruct((GROUP, 40, B), F32),
        ),
        out_specs=(hbm, pl.BlockSpec(memory_space=pltpu.VMEM)),
        scratch_shapes=[
            pltpu.VMEM((head_weight.shape[0], hp_local), BF16),
            pltpu.SemaphoreType.DMA(()),
        ],
        compiler_params=small_grant(8),
        name="heads",
    )(parts, features, head_weight, proj, fold)
    share = lax.all_to_all(share, ("x", "core"), 0, 0, tiled=True)
    share = pl.pallas_call(
        add_copies,
        out_shape=jax.ShapeDtypeStruct(share.shape, F32),
        compiler_params=small_grant(2),
        name="add_copies",
    )(near(share))
    share = lax.all_to_all(share, "y", 0, 0, tiled=True)
    grad_scale = float(hp_local * NSPACE) ** (-0.5)
    weight_grad = pl.pallas_call(
        functools.partial(add_last, grad_scale),
        out_shape=jax.ShapeDtypeStruct(head_weight.shape, F32),
        compiler_params=small_grant(2),
        name="add_last",
    )(near(share))
    return feature_grad, weight_grad


def solution(mesh):
    fine = Mesh(mesh.devices.reshape(NCHAN, 8, 4, 2), ("chan",) + SPACE)
    placed = (
        P(None, SPACE),
        P(SPACE),
        P(SPACE),
        P(SPACE),
        P(SPACE, None, None),
        P("chan", None),
        P("chan", SPACE),
    )
    return jax.shard_map(
        on_device,
        mesh=fine,
        in_specs=placed,
        out_specs=(P("chan", SPACE), P("chan", None)),
        check_vma=False,
    )
```

```python
import functools

import jax
import jax.numpy as jnp
import numpy as np
from jax import lax
from jax.experimental import pallas as pl
from jax.experimental.pallas import tpu as pltpu
from jax.sharding import Mesh
from jax.sharding import PartitionSpec as P

NCHAN = 8
NSPACE = 64
VARS = 80
B = 128
SLOTS = 128
BLOCKS = 16
OWN = VARS // NCHAN
MSG = 22
CHUNK = 32
PART = OWN * BLOCKS
GROUP = 8
SPACE = ("y", "x", "core")
F32 = jnp.float32
BF16 = jnp.bfloat16


def contribute(
    place, count, band_in, target_in, cot_in, weight_in, out,
    band, target, cot, weight, lhs, acc, seen, sems,
):
    chunks = SLOTS // CHUNK
    small = [
        pltpu.make_async_copy(src, dst, sems.at[chunks + k])
        for k, (src, dst) in enumerate(
            ((cot_in, cot), (band_in, band), (target_in, target))
        )
    ]

    def part(k):
        at = pl.ds(pl.multiple_of(k * CHUNK, CHUNK), CHUNK)
        return pltpu.make_async_copy(weight_in.at[at], weight.at[at], sems.at[k])

    for copy in small:
        copy.start()
    live_slots = count[0]
    groups = (live_slots + (CHUNK - 1)) // CHUNK
    for k in range(chunks):

        @pl.when(k < groups)
        def _():
            part(k).start()

    mine = place[0] // NSPACE
    space = place[0] % NSPACE
    for j in range(NSPACE):
        seen[j] = 2 * j
    row = lax.broadcasted_iota(jnp.int32, (32, VARS), 0)
    col = lax.broadcasted_iota(jnp.int32, (32, VARS), 1)
    low = row & 15
    tail = low - 8 - 2 * (row >> 4)
    var = jnp.where(low < 8, low, jnp.where((tail >= 0) & (tail < 2), 8 + tail, -VARS * NCHAN))
    pick = jnp.where(col == var + mine * OWN, 1.0, 0.0).astype(BF16)
    tag_row = lax.broadcasted_iota(jnp.int32, (8, B), 0)
    tag_lane = lax.broadcasted_iota(jnp.int32, (8, B), 1)
    tag_lane = jnp.where(tag_row == 4, tag_lane - 2 * space, -1)
    dead = 2 * BLOCKS
    lhs[dead] = jnp.zeros((16, B), BF16)
    acc[...] = jnp.zeros_like(acc)
    small[0].wait()
    rows = jnp.dot(pick, cot[...], preferred_element_type=F32).astype(BF16)
    for j in range(BLOCKS):
        for rank in range(2):
            lhs[2 * j + rank] = rows[16 * rank : 16 * rank + 16, j * B : (j + 1) * B]
    for copy in small[1:]:
        copy.wait()

    def chunk(k, carry):
        part(k).wait()
        for i in range(CHUNK):
            slot = k * CHUNK + i
            goal = target[slot]
            dest = goal >> 4
            key = seen[dest]
            seen[dest] = key + 1
            rank = key & 1
            live = slot < live_slots
            source = jnp.where(live, 2 * band[slot] + rank, dead)
            tag = jnp.where(live, (goal & 15) + 1, 0)
            value = jnp.dot(lhs[source], weight[slot], preferred_element_type=F32)
            acc[key, 0:8, :] = value[0:8]
            acc[key, 8:16, :] = value[8:16] + jnp.where(tag_lane == rank, tag, 0).astype(F32)
        return carry

    lax.fori_loop(0, groups, chunk, 0)

    sub = lax.broadcasted_iota(jnp.int32, (8, B), 0)

    def emit(k, carry):
        tiles = []
        for quad in range(2):
            first, second, extra, turned = [], [], [], []
            for h in range(4):
                one, two = acc[16 * k + 8 * quad + 2 * h], acc[16 * k + 8 * quad + 2 * h + 1]
                first.append(one[0:8])
                second.append(two[0:8])
                extra.append(one[8:16] + two[8:16])
                turned.append(pltpu.roll(extra[h], 2, 0))
            for h in range(4):
                tiles += [first[h], second[h]]
                if h < 3:
                    tiles.append(jnp.where(sub < 6 - 2 * h, extra[h], turned[h + 1]))
        rows = jnp.concatenate(tiles, axis=0).astype(BF16)
        out[pl.ds(pl.multiple_of(8 * MSG * k, 8 * MSG), 8 * MSG), :] = rows
        return carry

    lax.fori_loop(0, NSPACE // 8, emit, 0)


def collect(place, got, col, out):
    x = got[...]
    columns = NSPACE * MSG
    turn = (2 * (place[0] & 3)).astype(F32)
    at = col[0:1] - turn
    at = jnp.where(at < 0, at + MSG, at)
    src = col[1:2]
    main = at < 15.5
    rank = jnp.where(main, jnp.where(at < 7.5, 0.0, 1.0), jnp.where(at < 17.5, 0.0, 1.0))
    slot = jnp.where(at < 19.5, 2 * src + rank, -1.0)
    row = lax.broadcasted_iota(jnp.int32, (PART, columns), 0).astype(F32)
    spread = jnp.where(row[0:SLOTS] == slot, 1.0, 0.0).astype(BF16)
    tag_row = jnp.where(jnp.abs(at - 20) < 0.5, 0.0, -1.0)
    tag_pick = jnp.where(row[0:16] == tag_row, 1.0, 0.0).astype(BF16)
    tags = jnp.dot(tag_pick, x, preferred_element_type=F32).astype(BF16)
    label = jnp.dot(tags, spread, preferred_element_type=F32)[0:1]
    goal = jnp.where(main, 8 * label + (24 + at - 8 * rank), 2 * label + (at - 18 - 2 * rank))
    goal = jnp.where(label > 0.5, goal, -1.0)
    route = jnp.where(row == goal, 1.0, 0.0).astype(BF16)
    part = jnp.dot(route, x, preferred_element_type=F32).astype(BF16)
    for j in range(NCHAN):
        out[j] = part


def heads(parts, features, head, proj, fold, grad, share):
    def gather(at):
        return jnp.concatenate(
            [parts[PART * c + at : PART * c + at + 16] for c in range(NCHAN)], axis=0
        )

    tails = [gather(16 * k) for k in range(2)]
    mains = [gather(32 + 16 * k) for k in range(8)]
    lane = lax.broadcasted_iota(jnp.int32, (64, B), 1) & 15
    lifted = jnp.dot(head[...], proj[...], preferred_element_type=F32)
    low = [jnp.where((lane >> 3) == k, lifted[:, 0:B], 0.0).astype(BF16) for k in range(2)]
    high = [jnp.where((lane >> 1) == k, lifted[:, B:], 0.0).astype(BF16) for k in range(8)]
    for pair in range(BLOCKS // 2):
        left = jnp.concatenate(
            [
                jnp.concatenate([low[k], high[(2 * pair + k) % 8]], axis=1)
                for k in range(2)
            ],
            axis=0,
        )
        right = jnp.concatenate([mains[pair], tails[pair // 4]], axis=0)
        both = jnp.dot(left, right, preferred_element_type=F32).astype(BF16)
        for k in range(2):
            grad[:, (2 * pair + k) * B : (2 * pair + k + 1) * B] = both[64 * k : 64 * k + 64]

    def block(b):
        return features[:, b * B : (b + 1) * B]

    def product(left, right):
        return lax.dot_general(left, right, (((1,), (1,)), ((), ())), preferred_element_type=F32)

    paired = [
        jnp.concatenate([block(2 * k + half) for k in range(8)], axis=1) for half in range(2)
    ]
    total_main = product(jnp.concatenate(paired, axis=0), jnp.concatenate(mains, axis=1))
    eight = [jnp.concatenate([block(k), block(8 + k)], axis=1) for k in range(8)]
    total_tail = product(jnp.concatenate(eight, axis=0), jnp.concatenate(tails, axis=1))
    main = jnp.where((lane >> 3) == 0, total_main[0:64], total_main[64:128])
    tail = total_tail[0:64]
    for k in range(1, 8):
        tail = jnp.where((lane >> 1) == k, total_tail[64 * k : 64 * k + 64], tail)
    total = jnp.dot(
        jnp.concatenate([main, tail], axis=1),
        fold[...],
        preferred_element_type=F32,
        precision=lax.Precision.HIGHEST,
    )
    full = lax.broadcasted_iota(jnp.int32, (64, B), 1)
    first = jnp.where(full < 64, total, 0.0)
    rest = jnp.where(full < 64, 0.0, total)
    front = first[0:32] + pltpu.roll(first[32:64], 64, 1)
    back = rest[32:40]
    for k in range(8):
        if k != 4:
            back = back + pltpu.roll(rest[8 * k : 8 * k + 8], (16 * k - 64) % B, 1)
    for j in range(GROUP):
        share[j, 0:32] = front
        share[j, 32:40] = back


def add_up(got):
    total = got[0]
    for j in range(1, GROUP):
        total = total + got[j]
    return total


def add_copies(got, out):
    total = add_up(got)
    for j in range(GROUP):
        out[j] = total


def add_last(scale, got, grad, out, grad_out, sem):
    copy = pltpu.make_async_copy(grad, grad_out, sem)
    copy.start()
    total = add_up(got) * scale
    front, back = total[0:32], total[32:40]
    out[0:32, 0:64] = front[:, 0:64]
    out[32:64, 0:64] = pltpu.roll(front, 64, 1)[:, 0:64]
    for k in range(8):
        out[8 * k : 8 * k + 8, 64:VARS] = pltpu.roll(back, (64 - 16 * k) % B, 1)[:, 64:VARS]
    copy.wait()


def tables():
    j = np.arange(NSPACE * MSG)
    col = np.zeros((8, j.size), np.float32)
    col[0] = j % MSG
    col[1] = j // MSG
    k = np.arange(256)
    c, i = (k % 128) // 16, k % 16
    var = OWN * c + np.where(k < 128, i % 8, 8 + i % 2)
    proj = np.arange(VARS)[:, None] == var[None]
    fold = var[:, None] == np.arange(B)[None]
    return col, proj.astype(BF16), fold.astype(np.float32)


def small_grant(mib):
    return pltpu.CompilerParams(vmem_limit_bytes=mib << 20)


def near(x):
    return pltpu.with_memory_space_constraint(x, pltpu.VMEM)


def far(x):
    return pltpu.with_memory_space_constraint(x, pltpu.HBM)


def on_device(cotangent, pair_band, pair_target, pair_count, pair_weight, head_weight, features):
    col, proj, fold = tables()
    hp_local = features.shape[1]
    place = lax.axis_index(("chan",) + SPACE).astype(jnp.int32).reshape(1)
    hbm = pl.BlockSpec(memory_space=pltpu.HBM)
    sent = pl.pallas_call(
        contribute,
        out_shape=jax.ShapeDtypeStruct((NSPACE * MSG, B), BF16),
        in_specs=[pl.BlockSpec(memory_space=pltpu.SMEM)] * 2 + [hbm] * 4,
        scratch_shapes=[
            pltpu.SMEM((SLOTS,), jnp.int32),
            pltpu.SMEM((SLOTS,), jnp.int32),
            pltpu.VMEM((VARS, BLOCKS * B), BF16),
            pltpu.VMEM((SLOTS, B, B), BF16),
            pltpu.VMEM((2 * BLOCKS + 1, 16, B), BF16),
            pltpu.VMEM((SLOTS, 16, B), F32),
            pltpu.SMEM((NSPACE,), jnp.int32),
            pltpu.SemaphoreType.DMA((SLOTS // CHUNK + 3,)),
        ],
        compiler_params=small_grant(12),
        name="contribute",
    )(place, pair_count, *map(far, (pair_band, pair_target, cotangent, pair_weight)))
    got = lax.all_to_all(sent.reshape(NSPACE, MSG // 2, 2, B), SPACE, 0, 0, tiled=True)
    parts = pl.pallas_call(
        collect,
        out_shape=jax.ShapeDtypeStruct((NCHAN, PART, B), BF16),
        in_specs=[pl.BlockSpec(memory_space=pltpu.SMEM)]
        + [pl.BlockSpec(memory_space=pltpu.VMEM)] * 2,
        compiler_params=small_grant(8),
        name="collect",
    )(place, near(got.reshape(NSPACE * MSG, B)), col)
    parts = lax.all_to_all(parts, "chan", 0, 0, tiled=True).reshape(NCHAN * PART, B)
    parts = near(parts)
    feature_grad, share = pl.pallas_call(
        heads,
        out_shape=(
            jax.ShapeDtypeStruct((head_weight.shape[0], hp_local), BF16),
            jax.ShapeDtypeStruct((GROUP, 40, B), F32),
        ),
        out_specs=(pl.BlockSpec(memory_space=pltpu.VMEM),) * 2,
        compiler_params=small_grant(8),
        name="heads",
    )(parts, features, head_weight, proj, fold)
    share = lax.all_to_all(share, ("x", "core"), 0, 0, tiled=True)
    share = pl.pallas_call(
        add_copies,
        out_shape=jax.ShapeDtypeStruct(share.shape, F32),
        compiler_params=small_grant(2),
        name="add_copies",
    )(near(share))
    share = lax.all_to_all(share, "y", 0, 0, tiled=True)
    grad_scale = float(hp_local * NSPACE) ** (-0.5)
    weight_grad, feature_grad = pl.pallas_call(
        functools.partial(add_last, grad_scale),
        out_shape=(
            jax.ShapeDtypeStruct(head_weight.shape, F32),
            jax.ShapeDtypeStruct(feature_grad.shape, BF16),
        ),
        out_specs=(pl.BlockSpec(memory_space=pltpu.VMEM), hbm),
        scratch_shapes=[pltpu.SemaphoreType.DMA(())],
        compiler_params=small_grant(2),
        name="add_last",
    )(near(share), near(feature_grad))
    return feature_grad, weight_grad


def solution(mesh):
    fine = Mesh(mesh.devices.reshape(NCHAN, 8, 4, 2), ("chan",) + SPACE)
    placed = (
        P(None, SPACE),
        P(SPACE),
        P(SPACE),
        P(SPACE),
        P(SPACE, None, None),
        P("chan", None),
        P("chan", SPACE),
    )
    return jax.shard_map(
        on_device,
        mesh=fine,
        in_specs=placed,
        out_specs=(P("chan", SPACE), P("chan", None)),
        check_vma=False,
    )
```

```python
import functools

import jax
import jax.numpy as jnp
import numpy as np
from jax import lax
from jax.experimental import pallas as pl
from jax.experimental.pallas import tpu as pltpu
from jax.sharding import Mesh
from jax.sharding import PartitionSpec as P

NCHAN = 8
NSPACE = 64
VARS = 80
B = 128
SLOTS = 128
BLOCKS = 16
OWN = VARS // NCHAN
MSG = 22
CHUNK = 32
PART = OWN * BLOCKS
GROUP = 8
SPACE = ("y", "x", "core")
F32 = jnp.float32
BF16 = jnp.bfloat16


def contribute(
    place, count, band_in, target_in, cot_in, weight_in, out,
    band, target, cot, weight, lhs, acc, seen, sems,
):
    chunks = SLOTS // CHUNK
    small = [
        pltpu.make_async_copy(src, dst, sems.at[chunks + k])
        for k, (src, dst) in enumerate(
            ((cot_in, cot), (band_in, band), (target_in, target))
        )
    ]

    def part(k):
        at = pl.ds(pl.multiple_of(k * CHUNK, CHUNK), CHUNK)
        return pltpu.make_async_copy(weight_in.at[at], weight.at[at], sems.at[k])

    for copy in small:
        copy.start()
    live_slots = count[0]
    groups = (live_slots + (CHUNK - 1)) // CHUNK
    for k in range(chunks):

        @pl.when(k < groups)
        def _():
            part(k).start()

    mine = place[0] // NSPACE
    space = place[0] % NSPACE
    for j in range(NSPACE):
        seen[j] = 2 * j
    row = lax.broadcasted_iota(jnp.int32, (32, VARS), 0)
    col = lax.broadcasted_iota(jnp.int32, (32, VARS), 1)
    low = row & 15
    tail = low - 8 - 2 * (row >> 4)
    var = jnp.where(low < 8, low, jnp.where((tail >= 0) & (tail < 2), 8 + tail, -VARS * NCHAN))
    pick = jnp.where(col == var + mine * OWN, 1.0, 0.0).astype(BF16)
    tag_row = lax.broadcasted_iota(jnp.int32, (8, B), 0)
    tag_lane = lax.broadcasted_iota(jnp.int32, (8, B), 1)
    tag_lane = jnp.where(tag_row == 4, tag_lane - 2 * space, -1)
    dead = 2 * BLOCKS
    lhs[dead] = jnp.zeros((16, B), BF16)
    acc[...] = jnp.zeros_like(acc)
    small[0].wait()
    rows = jnp.dot(pick, cot[...], preferred_element_type=F32).astype(BF16)
    for j in range(BLOCKS):
        for rank in range(2):
            lhs[2 * j + rank] = rows[16 * rank : 16 * rank + 16, j * B : (j + 1) * B]
    for copy in small[1:]:
        copy.wait()

    def chunk(k, carry):
        part(k).wait()
        for i in range(CHUNK):
            slot = k * CHUNK + i
            goal = target[slot]
            dest = goal >> 4
            key = seen[dest]
            seen[dest] = key + 1
            rank = key & 1
            live = slot < live_slots
            source = jnp.where(live, 2 * band[slot] + rank, dead)
            tag = jnp.where(live, (goal & 15) + 1, 0)
            value = jnp.dot(lhs[source], weight[slot], preferred_element_type=F32)
            acc[key, 0:8, :] = value[0:8]
            acc[key, 8:16, :] = value[8:16] + jnp.where(tag_lane == rank, tag, 0).astype(F32)
        return carry

    lax.fori_loop(0, groups, chunk, 0)

    sub = lax.broadcasted_iota(jnp.int32, (8, B), 0)

    def emit(k, carry):
        tiles = []
        for quad in range(2):
            first, second, extra, turned = [], [], [], []
            for h in range(4):
                one, two = acc[16 * k + 8 * quad + 2 * h], acc[16 * k + 8 * quad + 2 * h + 1]
                first.append(one[0:8])
                second.append(two[0:8])
                extra.append(one[8:16] + two[8:16])
                turned.append(pltpu.roll(extra[h], 2, 0))
            for h in range(4):
                tiles += [first[h], second[h]]
                if h < 3:
                    tiles.append(jnp.where(sub < 6 - 2 * h, extra[h], turned[h + 1]))
        rows = jnp.concatenate(tiles, axis=0).astype(BF16)
        out[pl.ds(pl.multiple_of(8 * MSG * k, 8 * MSG), 8 * MSG), :] = rows
        return carry

    lax.fori_loop(0, NSPACE // 8, emit, 0)


def collect(place, got, col, out):
    x = got[...]
    columns = NSPACE * MSG
    turn = (2 * (place[0] & 3)).astype(F32)
    at = col[0:1] - turn
    at = jnp.where(at < 0, at + MSG, at)
    src = col[1:2]
    main = at < 15.5
    rank = jnp.where(main, jnp.where(at < 7.5, 0.0, 1.0), jnp.where(at < 17.5, 0.0, 1.0))
    slot = jnp.where(at < 19.5, 2 * src + rank, -1.0)
    row = lax.broadcasted_iota(jnp.int32, (PART, columns), 0).astype(F32)
    spread = jnp.where(row[0:SLOTS] == slot, 1.0, 0.0).astype(BF16)
    tag_row = jnp.where(jnp.abs(at - 20) < 0.5, 0.0, -1.0)
    tag_pick = jnp.where(row[0:16] == tag_row, 1.0, 0.0).astype(BF16)
    tags = jnp.dot(tag_pick, x, preferred_element_type=F32).astype(BF16)
    label = jnp.dot(tags, spread, preferred_element_type=F32)[0:1]
    goal = jnp.where(main, 8 * label + (24 + at - 8 * rank), 2 * label + (at - 18 - 2 * rank))
    goal = jnp.where(label > 0.5, goal, -1.0)
    route = jnp.where(row == goal, 1.0, 0.0).astype(BF16)
    part = jnp.dot(route, x, preferred_element_type=F32).astype(BF16)
    for j in range(NCHAN):
        out[j] = part


def heads(parts, features, head, proj, fold, grad_out, share, grad, sem):
    def gather(at):
        return jnp.concatenate(
            [parts[PART * c + at : PART * c + at + 16] for c in range(NCHAN)], axis=0
        )

    tails = [gather(16 * k) for k in range(2)]
    mains = [gather(32 + 16 * k) for k in range(8)]
    lane = lax.broadcasted_iota(jnp.int32, (64, B), 1) & 15
    lifted = jnp.dot(head[...], proj[...], preferred_element_type=F32)
    low = [jnp.where((lane >> 3) == k, lifted[:, 0:B], 0.0).astype(BF16) for k in range(2)]
    high = [jnp.where((lane >> 1) == k, lifted[:, B:], 0.0).astype(BF16) for k in range(8)]
    copies = []
    for pair in range(BLOCKS // 2):
        left = jnp.concatenate(
            [
                jnp.concatenate([low[k], high[(2 * pair + k) % 8]], axis=1)
                for k in range(2)
            ],
            axis=0,
        )
        right = jnp.concatenate([mains[pair], tails[pair // 4]], axis=0)
        both = jnp.dot(left, right, preferred_element_type=F32).astype(BF16)
        for k in range(2):
            grad[:, (2 * pair + k) * B : (2 * pair + k + 1) * B] = both[64 * k : 64 * k + 64]
        if pair % 2:
            at = pl.ds((2 * pair - 2) * B, 4 * B)
            copies.append(
                pltpu.make_async_copy(grad.at[:, at], grad_out.at[:, at], sem.at[pair // 2])
            )
            copies[-1].start()

    def block(b):
        return features[:, b * B : (b + 1) * B]

    def product(left, right):
        return lax.dot_general(left, right, (((1,), (1,)), ((), ())), preferred_element_type=F32)

    paired = [
        jnp.concatenate([block(2 * k + half) for k in range(8)], axis=1) for half in range(2)
    ]
    total_main = product(jnp.concatenate(paired, axis=0), jnp.concatenate(mains, axis=1))
    eight = [jnp.concatenate([block(k), block(8 + k)], axis=1) for k in range(8)]
    total_tail = product(jnp.concatenate(eight, axis=0), jnp.concatenate(tails, axis=1))
    main = jnp.where((lane >> 3) == 0, total_main[0:64], total_main[64:128])
    tail = total_tail[0:64]
    for k in range(1, 8):
        tail = jnp.where((lane >> 1) == k, total_tail[64 * k : 64 * k + 64], tail)
    total = jnp.dot(
        jnp.concatenate([main, tail], axis=1),
        fold[...],
        preferred_element_type=F32,
        precision=lax.Precision.HIGHEST,
    )
    full = lax.broadcasted_iota(jnp.int32, (64, B), 1)
    first = jnp.where(full < 64, total, 0.0)
    rest = jnp.where(full < 64, 0.0, total)
    front = first[0:32] + pltpu.roll(first[32:64], 64, 1)
    back = rest[32:40]
    for k in range(8):
        if k != 4:
            back = back + pltpu.roll(rest[8 * k : 8 * k + 8], (16 * k - 64) % B, 1)
    for j in range(GROUP):
        share[j, 0:32] = front
        share[j, 32:40] = back
    for copy in copies:
        copy.wait()


def add_up(got):
    total = got[0]
    for j in range(1, GROUP):
        total = total + got[j]
    return total


def add_copies(got, out):
    total = add_up(got)
    for j in range(GROUP):
        out[j] = total


def add_last(scale, got, out):
    total = add_up(got) * scale
    front, back = total[0:32], total[32:40]
    out[0:32, 0:64] = front[:, 0:64]
    out[32:64, 0:64] = pltpu.roll(front, 64, 1)[:, 0:64]
    for k in range(8):
        out[8 * k : 8 * k + 8, 64:VARS] = pltpu.roll(back, (64 - 16 * k) % B, 1)[:, 64:VARS]


def tables():
    j = np.arange(NSPACE * MSG)
    col = np.zeros((8, j.size), np.float32)
    col[0] = j % MSG
    col[1] = j // MSG
    k = np.arange(256)
    c, i = (k % 128) // 16, k % 16
    var = OWN * c + np.where(k < 128, i % 8, 8 + i % 2)
    proj = np.arange(VARS)[:, None] == var[None]
    fold = var[:, None] == np.arange(B)[None]
    return col, proj.astype(BF16), fold.astype(np.float32)


def small_grant(mib):
    return pltpu.CompilerParams(vmem_limit_bytes=mib << 20)


def near(x):
    return pltpu.with_memory_space_constraint(x, pltpu.VMEM)


def far(x):
    return pltpu.with_memory_space_constraint(x, pltpu.HBM)


def on_device(cotangent, pair_band, pair_target, pair_count, pair_weight, head_weight, features):
    col, proj, fold = tables()
    hp_local = features.shape[1]
    place = lax.axis_index(("chan",) + SPACE).astype(jnp.int32).reshape(1)
    hbm = pl.BlockSpec(memory_space=pltpu.HBM)
    sent = pl.pallas_call(
        contribute,
        out_shape=jax.ShapeDtypeStruct((NSPACE * MSG, B), BF16),
        in_specs=[pl.BlockSpec(memory_space=pltpu.SMEM)] * 2 + [hbm] * 4,
        scratch_shapes=[
            pltpu.SMEM((SLOTS,), jnp.int32),
            pltpu.SMEM((SLOTS,), jnp.int32),
            pltpu.VMEM((VARS, BLOCKS * B), BF16),
            pltpu.VMEM((SLOTS, B, B), BF16),
            pltpu.VMEM((2 * BLOCKS + 1, 16, B), BF16),
            pltpu.VMEM((SLOTS, 16, B), F32),
            pltpu.SMEM((NSPACE,), jnp.int32),
            pltpu.SemaphoreType.DMA((SLOTS // CHUNK + 3,)),
        ],
        compiler_params=small_grant(12),
        name="contribute",
    )(place, pair_count, *map(far, (pair_band, pair_target, cotangent, pair_weight)))
    got = lax.all_to_all(sent.reshape(NSPACE, MSG // 2, 2, B), SPACE, 0, 0, tiled=True)
    parts = pl.pallas_call(
        collect,
        out_shape=jax.ShapeDtypeStruct((NCHAN, PART, B), BF16),
        in_specs=[pl.BlockSpec(memory_space=pltpu.SMEM)]
        + [pl.BlockSpec(memory_space=pltpu.VMEM)] * 2,
        compiler_params=small_grant(8),
        name="collect",
    )(place, near(got.reshape(NSPACE * MSG, B)), col)
    parts = lax.all_to_all(parts, "chan", 0, 0, tiled=True).reshape(NCHAN * PART, B)
    parts = near(parts)
    feature_grad, share = pl.pallas_call(
        heads,
        out_shape=(
            jax.ShapeDtypeStruct((head_weight.shape[0], hp_local), BF16),
            jax.ShapeDtypeStruct((GROUP, 40, B), F32),
        ),
        out_specs=(hbm, pl.BlockSpec(memory_space=pltpu.VMEM)),
        scratch_shapes=[
            pltpu.VMEM((head_weight.shape[0], hp_local), BF16),
            pltpu.SemaphoreType.DMA((4,)),
        ],
        compiler_params=small_grant(8),
        name="heads",
    )(parts, features, head_weight, proj, fold)
    share = lax.all_to_all(share, "y", 0, 0, tiled=True)
    share = pl.pallas_call(
        add_copies,
        out_shape=jax.ShapeDtypeStruct(share.shape, F32),
        compiler_params=small_grant(2),
        name="add_copies",
    )(near(share))
    share = lax.all_to_all(share, ("x", "core"), 0, 0, tiled=True)
    grad_scale = float(hp_local * NSPACE) ** (-0.5)
    weight_grad = pl.pallas_call(
        functools.partial(add_last, grad_scale),
        out_shape=jax.ShapeDtypeStruct(head_weight.shape, F32),
        compiler_params=small_grant(2),
        name="add_last",
    )(near(share))
    return feature_grad, weight_grad


def solution(mesh):
    fine = Mesh(mesh.devices.reshape(NCHAN, 8, 4, 2), ("chan",) + SPACE)
    placed = (
        P(None, SPACE),
        P(SPACE),
        P(SPACE),
        P(SPACE),
        P(SPACE, None, None),
        P("chan", None),
        P("chan", SPACE),
    )
    return jax.shard_map(
        on_device,
        mesh=fine,
        in_specs=placed,
        out_specs=(P("chan", SPACE), P("chan", None)),
        check_vma=False,
    )
```

```python
import functools

import jax
import jax.numpy as jnp
import numpy as np
from jax import lax
from jax.experimental import pallas as pl
from jax.experimental.pallas import tpu as pltpu
from jax.sharding import Mesh
from jax.sharding import PartitionSpec as P

NCHAN = 8
NSPACE = 64
VARS = 80
B = 128
SLOTS = 128
BLOCKS = 16
OWN = VARS // NCHAN
MSG = 22
CHUNK = 16
PART = OWN * BLOCKS
GROUP = 8
SPACE = ("y", "x", "core")
F32 = jnp.float32
BF16 = jnp.bfloat16


def contribute(
    place, count, band_in, target_in, cot_in, weight_in, out,
    band, target, cot, weight, lhs, acc, seen, sems,
):
    chunks = SLOTS // CHUNK
    small = [
        pltpu.make_async_copy(src, dst, sems.at[chunks + k])
        for k, (src, dst) in enumerate(
            ((cot_in, cot), (band_in, band), (target_in, target))
        )
    ]

    def part(k):
        at = pl.ds(pl.multiple_of(k * CHUNK, CHUNK), CHUNK)
        return pltpu.make_async_copy(weight_in.at[at], weight.at[at], sems.at[k])

    for copy in small:
        copy.start()
    live_slots = count[0]
    groups = (live_slots + (CHUNK - 1)) // CHUNK
    for k in range(chunks):

        @pl.when(k < groups)
        def _():
            part(k).start()

    mine = place[0] // NSPACE
    space = place[0] % NSPACE
    for j in range(NSPACE):
        seen[j] = 2 * j
    row = lax.broadcasted_iota(jnp.int32, (32, VARS), 0)
    col = lax.broadcasted_iota(jnp.int32, (32, VARS), 1)
    low = row & 15
    tail = low - 8 - 2 * (row >> 4)
    var = jnp.where(low < 8, low, jnp.where((tail >= 0) & (tail < 2), 8 + tail, -VARS * NCHAN))
    pick = jnp.where(col == var + mine * OWN, 1.0, 0.0).astype(BF16)
    tag_row = lax.broadcasted_iota(jnp.int32, (8, B), 0)
    tag_lane = lax.broadcasted_iota(jnp.int32, (8, B), 1)
    tag_lane = jnp.where(tag_row == 4, tag_lane - 2 * space, -1)
    dead = 2 * BLOCKS
    lhs[dead] = jnp.zeros((16, B), BF16)
    acc[...] = jnp.zeros_like(acc)
    small[0].wait()
    rows = jnp.dot(pick, cot[...], preferred_element_type=F32).astype(BF16)
    for j in range(BLOCKS):
        for rank in range(2):
            lhs[2 * j + rank] = rows[16 * rank : 16 * rank + 16, j * B : (j + 1) * B]
    for copy in small[1:]:
        copy.wait()

    def chunk(k, carry):
        part(k).wait()
        for i in range(CHUNK):
            slot = k * CHUNK + i
            goal = target[slot]
            dest = goal >> 4
            key = seen[dest]
            seen[dest] = key + 1
            rank = key & 1
            live = slot < live_slots
            source = jnp.where(live, 2 * band[slot] + rank, dead)
            tag = jnp.where(live, (goal & 15) + 1, 0)
            value = jnp.dot(lhs[source], weight[slot], preferred_element_type=F32)
            acc[key, 0:8, :] = value[0:8]
            acc[key, 8:16, :] = value[8:16] + jnp.where(tag_lane == rank, tag, 0).astype(F32)
        return carry

    lax.fori_loop(0, groups, chunk, 0)

    sub = lax.broadcasted_iota(jnp.int32, (8, B), 0)

    def emit(k, carry):
        tiles = []
        for quad in range(2):
            first, second, extra, turned = [], [], [], []
            for h in range(4):
                one, two = acc[16 * k + 8 * quad + 2 * h], acc[16 * k + 8 * quad + 2 * h + 1]
                first.append(one[0:8])
                second.append(two[0:8])
                extra.append(one[8:16] + two[8:16])
                turned.append(pltpu.roll(extra[h], 2, 0))
            for h in range(4):
                tiles += [first[h], second[h]]
                if h < 3:
                    tiles.append(jnp.where(sub < 6 - 2 * h, extra[h], turned[h + 1]))
        rows = jnp.concatenate(tiles, axis=0).astype(BF16)
        out[pl.ds(pl.multiple_of(8 * MSG * k, 8 * MSG), 8 * MSG), :] = rows
        return carry

    lax.fori_loop(0, NSPACE // 8, emit, 0)


def collect(place, got, col, out):
    x = got[...]
    columns = NSPACE * MSG
    turn = (2 * (place[0] & 3)).astype(F32)
    at = col[0:1] - turn
    at = jnp.where(at < 0, at + MSG, at)
    src = col[1:2]
    main = at < 15.5
    rank = jnp.where(main, jnp.where(at < 7.5, 0.0, 1.0), jnp.where(at < 17.5, 0.0, 1.0))
    slot = jnp.where(at < 19.5, 2 * src + rank, -1.0)
    row = lax.broadcasted_iota(jnp.int32, (PART, columns), 0).astype(F32)
    spread = jnp.where(row[0:SLOTS] == slot, 1.0, 0.0).astype(BF16)
    tag_row = jnp.where(jnp.abs(at - 20) < 0.5, 0.0, -1.0)
    tag_pick = jnp.where(row[0:16] == tag_row, 1.0, 0.0).astype(BF16)
    tags = jnp.dot(tag_pick, x, preferred_element_type=F32).astype(BF16)
    label = jnp.dot(tags, spread, preferred_element_type=F32)[0:1]
    goal = jnp.where(main, 8 * label + (24 + at - 8 * rank), 2 * label + (at - 18 - 2 * rank))
    goal = jnp.where(label > 0.5, goal, -1.0)
    route = jnp.where(row == goal, 1.0, 0.0).astype(BF16)
    part = jnp.dot(route, x, preferred_element_type=F32).astype(BF16)
    for j in range(NCHAN):
        out[j] = part


def heads(parts, features, head, proj, fold, grad, share):
    def gather(at):
        return jnp.concatenate(
            [parts[PART * c + at : PART * c + at + 16] for c in range(NCHAN)], axis=0
        )

    tails = [gather(16 * k) for k in range(2)]
    mains = [gather(32 + 16 * k) for k in range(8)]
    lane = lax.broadcasted_iota(jnp.int32, (64, B), 1) & 15
    lifted = jnp.dot(head[...], proj[...], preferred_element_type=F32)
    low = [jnp.where((lane >> 3) == k, lifted[:, 0:B], 0.0).astype(BF16) for k in range(2)]
    high = [jnp.where((lane >> 1) == k, lifted[:, B:], 0.0).astype(BF16) for k in range(8)]
    for pair in range(BLOCKS // 2):
        left = jnp.concatenate(
            [
                jnp.concatenate([low[k], high[(2 * pair + k) % 8]], axis=1)
                for k in range(2)
            ],
            axis=0,
        )
        right = jnp.concatenate([mains[pair], tails[pair // 4]], axis=0)
        both = jnp.dot(left, right, preferred_element_type=F32).astype(BF16)
        for k in range(2):
            grad[:, (2 * pair + k) * B : (2 * pair + k + 1) * B] = both[64 * k : 64 * k + 64]

    def block(b):
        return features[:, b * B : (b + 1) * B]

    def product(left, right):
        return lax.dot_general(left, right, (((1,), (1,)), ((), ())), preferred_element_type=F32)

    paired = [
        jnp.concatenate([block(2 * k + half) for k in range(8)], axis=1) for half in range(2)
    ]
    total_main = product(jnp.concatenate(paired, axis=0), jnp.concatenate(mains, axis=1))
    eight = [jnp.concatenate([block(k), block(8 + k)], axis=1) for k in range(8)]
    total_tail = product(jnp.concatenate(eight, axis=0), jnp.concatenate(tails, axis=1))
    main = jnp.where((lane >> 3) == 0, total_main[0:64], total_main[64:128])
    tail = total_tail[0:64]
    for k in range(1, 8):
        tail = jnp.where((lane >> 1) == k, total_tail[64 * k : 64 * k + 64], tail)
    total = jnp.dot(
        jnp.concatenate([main, tail], axis=1),
        fold[...],
        preferred_element_type=F32,
        precision=lax.Precision.HIGHEST,
    )
    full = lax.broadcasted_iota(jnp.int32, (64, B), 1)
    first = jnp.where(full < 64, total, 0.0)
    rest = jnp.where(full < 64, 0.0, total)
    front = first[0:32] + pltpu.roll(first[32:64], 64, 1)
    back = rest[32:40]
    for k in range(8):
        if k != 4:
            back = back + pltpu.roll(rest[8 * k : 8 * k + 8], (16 * k - 64) % B, 1)
    for j in range(GROUP):
        share[j, 0:32] = front
        share[j, 32:40] = back


def add_up(got):
    total = got[0]
    for j in range(1, GROUP):
        total = total + got[j]
    return total


def add_copies(got, out):
    total = add_up(got)
    for j in range(GROUP):
        out[j] = total


def add_last(scale, got, grad, out, grad_out, sem):
    copies = [
        pltpu.make_async_copy(grad.at[8 * k : 8 * k + 8], grad_out.at[8 * k : 8 * k + 8], sem.at[k])
        for k in range(8)
    ]
    for copy in copies:
        copy.start()
    total = add_up(got) * scale
    front, back = total[0:32], total[32:40]
    out[0:32, 0:64] = front[:, 0:64]
    out[32:64, 0:64] = pltpu.roll(front, 64, 1)[:, 0:64]
    for k in range(8):
        out[8 * k : 8 * k + 8, 64:VARS] = pltpu.roll(back, (64 - 16 * k) % B, 1)[:, 64:VARS]
    for copy in copies:
        copy.wait()


def tables():
    j = np.arange(NSPACE * MSG)
    col = np.zeros((8, j.size), np.float32)
    col[0] = j % MSG
    col[1] = j // MSG
    k = np.arange(256)
    c, i = (k % 128) // 16, k % 16
    var = OWN * c + np.where(k < 128, i % 8, 8 + i % 2)
    proj = np.arange(VARS)[:, None] == var[None]
    fold = var[:, None] == np.arange(B)[None]
    return col, proj.astype(BF16), fold.astype(np.float32)


def small_grant(mib):
    return pltpu.CompilerParams(vmem_limit_bytes=mib << 20)


def near(x):
    return pltpu.with_memory_space_constraint(x, pltpu.VMEM)


def far(x):
    return pltpu.with_memory_space_constraint(x, pltpu.HBM)


def on_device(cotangent, pair_band, pair_target, pair_count, pair_weight, head_weight, features):
    col, proj, fold = tables()
    hp_local = features.shape[1]
    place = lax.axis_index(("chan",) + SPACE).astype(jnp.int32).reshape(1)
    hbm = pl.BlockSpec(memory_space=pltpu.HBM)
    sent = pl.pallas_call(
        contribute,
        out_shape=jax.ShapeDtypeStruct((NSPACE * MSG, B), BF16),
        in_specs=[pl.BlockSpec(memory_space=pltpu.SMEM)] * 2 + [hbm] * 4,
        scratch_shapes=[
            pltpu.SMEM((SLOTS,), jnp.int32),
            pltpu.SMEM((SLOTS,), jnp.int32),
            pltpu.VMEM((VARS, BLOCKS * B), BF16),
            pltpu.VMEM((SLOTS, B, B), BF16),
            pltpu.VMEM((2 * BLOCKS + 1, 16, B), BF16),
            pltpu.VMEM((SLOTS, 16, B), F32),
            pltpu.SMEM((NSPACE,), jnp.int32),
            pltpu.SemaphoreType.DMA((SLOTS // CHUNK + 3,)),
        ],
        compiler_params=small_grant(12),
        name="contribute",
    )(place, pair_count, *map(far, (pair_band, pair_target, cotangent, pair_weight)))
    got = lax.all_to_all(sent.reshape(NSPACE, MSG // 2, 2, B), SPACE, 0, 0, tiled=True)
    parts = pl.pallas_call(
        collect,
        out_shape=jax.ShapeDtypeStruct((NCHAN, PART, B), BF16),
        in_specs=[pl.BlockSpec(memory_space=pltpu.SMEM)]
        + [pl.BlockSpec(memory_space=pltpu.VMEM)] * 2,
        compiler_params=small_grant(8),
        name="collect",
    )(place, near(got.reshape(NSPACE * MSG, B)), col)
    parts = lax.all_to_all(parts, "chan", 0, 0, tiled=True).reshape(NCHAN * PART, B)
    parts = near(parts)
    feature_grad, share = pl.pallas_call(
        heads,
        out_shape=(
            jax.ShapeDtypeStruct((head_weight.shape[0], hp_local), BF16),
            jax.ShapeDtypeStruct((GROUP, 40, B), F32),
        ),
        out_specs=(pl.BlockSpec(memory_space=pltpu.VMEM),) * 2,
        compiler_params=small_grant(8),
        name="heads",
    )(parts, features, head_weight, proj, fold)
    share = lax.all_to_all(share, ("x", "core"), 0, 0, tiled=True)
    share = pl.pallas_call(
        add_copies,
        out_shape=jax.ShapeDtypeStruct(share.shape, F32),
        compiler_params=small_grant(2),
        name="add_copies",
    )(near(share))
    share = lax.all_to_all(share, "y", 0, 0, tiled=True)
    grad_scale = float(hp_local * NSPACE) ** (-0.5)
    weight_grad, feature_grad = pl.pallas_call(
        functools.partial(add_last, grad_scale),
        out_shape=(
            jax.ShapeDtypeStruct(head_weight.shape, F32),
            jax.ShapeDtypeStruct(feature_grad.shape, BF16),
        ),
        out_specs=(pl.BlockSpec(memory_space=pltpu.VMEM), hbm),
        scratch_shapes=[pltpu.SemaphoreType.DMA((8,))],
        compiler_params=small_grant(2),
        name="add_last",
    )(near(share), near(feature_grad))
    return feature_grad, weight_grad


def solution(mesh):
    fine = Mesh(mesh.devices.reshape(NCHAN, 8, 4, 2), ("chan",) + SPACE)
    placed = (
        P(None, SPACE),
        P(SPACE),
        P(SPACE),
        P(SPACE),
        P(SPACE, None, None),
        P("chan", None),
        P("chan", SPACE),
    )
    return jax.shard_map(
        on_device,
        mesh=fine,
        in_specs=placed,
        out_specs=(P("chan", SPACE), P("chan", None)),
        check_vma=False,
    )
```

```python
import functools

import jax
import jax.numpy as jnp
import numpy as np
from jax import lax
from jax.experimental import pallas as pl
from jax.experimental.pallas import tpu as pltpu
from jax.sharding import Mesh
from jax.sharding import PartitionSpec as P

NCHAN = 8
NSPACE = 64
VARS = 80
B = 128
SLOTS = 128
BLOCKS = 16
OWN = VARS // NCHAN
MSG = 22
CHUNK = 32
PART = OWN * BLOCKS
GROUP = 8
SPACE = ("y", "x", "core")
F32 = jnp.float32
BF16 = jnp.bfloat16


def contribute(
    place, count, band_in, target_in, cot_in, head_in, weight_in, out, tag_pick, spread, left,
    band, target, cot, head, weight, lhs, acc, seen, sems,
):
    chunks = SLOTS // CHUNK
    small = [
        pltpu.make_async_copy(src, dst, sems.at[chunks + k])
        for k, (src, dst) in enumerate(
            ((cot_in, cot), (band_in, band), (target_in, target), (head_in, head))
        )
    ]

    def part(k):
        at = pl.ds(pl.multiple_of(k * CHUNK, CHUNK), CHUNK)
        return pltpu.make_async_copy(weight_in.at[at], weight.at[at], sems.at[k])

    for copy in small:
        copy.start()
    live_slots = count[0]
    groups = (live_slots + (CHUNK - 1)) // CHUNK
    for k in range(chunks):

        @pl.when(k < groups)
        def _():
            part(k).start()

    mine = place[0] // NSPACE
    space = place[0] % NSPACE
    for j in range(NSPACE):
        seen[j] = 2 * j
    row = lax.broadcasted_iota(jnp.int32, (32, VARS), 0)
    col = lax.broadcasted_iota(jnp.int32, (32, VARS), 1)
    low = row & 15
    tail = low - 8 - 2 * (row >> 4)
    var = jnp.where(low < 8, low, jnp.where((tail >= 0) & (tail < 2), 8 + tail, -VARS * NCHAN))
    pick = jnp.where(col == var + mine * OWN, 1.0, 0.0).astype(BF16)
    tag_row = lax.broadcasted_iota(jnp.int32, (8, B), 0)
    tag_lane = lax.broadcasted_iota(jnp.int32, (8, B), 1)
    tag_lane = jnp.where(tag_row == 4, tag_lane - 2 * space, -1)
    dead = 2 * BLOCKS
    lhs[dead] = jnp.zeros((16, B), BF16)
    acc[...] = jnp.zeros_like(acc)
    at, src, _, rank = message_columns(place)
    lane = lax.broadcasted_iota(jnp.int32, (SLOTS, NSPACE * MSG), 0).astype(F32)
    slot_of = jnp.where(at < 19.5, 2 * src + rank, -1.0)
    spread[...] = jnp.where(lane == slot_of, 1.0, 0.0).astype(BF16)
    tag_row_of = jnp.where(jnp.abs(at - 20) < 0.5, 0.0, -1.0)
    tag_pick[...] = jnp.where(lane[0:16] == tag_row_of, 1.0, 0.0).astype(BF16)
    small[3].wait()
    left_operands(head, left)
    small[0].wait()
    rows = jnp.dot(pick, cot[...], preferred_element_type=F32).astype(BF16)
    for j in range(BLOCKS):
        for rank in range(2):
            lhs[2 * j + rank] = rows[16 * rank : 16 * rank + 16, j * B : (j + 1) * B]
    for copy in small[1:3]:
        copy.wait()

    def chunk(k, carry):
        part(k).wait()
        for i in range(CHUNK):
            slot = k * CHUNK + i
            goal = target[slot]
            dest = goal >> 4
            key = seen[dest]
            seen[dest] = key + 1
            rank = key & 1
            live = slot < live_slots
            source = jnp.where(live, 2 * band[slot] + rank, dead)
            tag = jnp.where(live, (goal & 15) + 1, 0)
            value = jnp.dot(lhs[source], weight[slot], preferred_element_type=F32)
            acc[key, 0:8, :] = value[0:8]
            acc[key, 8:16, :] = value[8:16] + jnp.where(tag_lane == rank, tag, 0).astype(F32)
        return carry

    lax.fori_loop(0, groups, chunk, 0)

    sub = lax.broadcasted_iota(jnp.int32, (8, B), 0)

    def emit(k, carry):
        tiles = []
        for quad in range(2):
            first, second, extra, turned = [], [], [], []
            for h in range(4):
                one, two = acc[16 * k + 8 * quad + 2 * h], acc[16 * k + 8 * quad + 2 * h + 1]
                first.append(one[0:8])
                second.append(two[0:8])
                extra.append(one[8:16] + two[8:16])
                turned.append(pltpu.roll(extra[h], 2, 0))
            for h in range(4):
                tiles += [first[h], second[h]]
                if h < 3:
                    tiles.append(jnp.where(sub < 6 - 2 * h, extra[h], turned[h + 1]))
        rows = jnp.concatenate(tiles, axis=0).astype(BF16)
        out[pl.ds(pl.multiple_of(8 * MSG * k, 8 * MSG), 8 * MSG), :] = rows
        return carry

    lax.fori_loop(0, NSPACE // 8, emit, 0)


def message_columns(place):
    j = lax.broadcasted_iota(jnp.int32, (1, NSPACE * MSG), 1).astype(F32)
    src = jnp.floor((j + 0.5) * (1.0 / MSG))
    at = j - MSG * src - (2 * (place[0] & 3)).astype(F32)
    at = jnp.where(at < 0, at + MSG, at)
    main = at < 15.5
    rank = jnp.where(main, jnp.where(at < 7.5, 0.0, 1.0), jnp.where(at < 17.5, 0.0, 1.0))
    return at, src, main, rank


def left_operands(head, left):
    var = lax.broadcasted_iota(jnp.int32, (VARS, 2 * B), 0)
    col = lax.broadcasted_iota(jnp.int32, (VARS, 2 * B), 1)
    own = jnp.where(col < B, col & 7, 8 + (col & 1))
    proj = jnp.where(var == OWN * ((col & (B - 1)) >> 4) + own, 1.0, 0.0).astype(BF16)
    lifted = jnp.dot(head[...], proj, preferred_element_type=F32)
    lane = lax.broadcasted_iota(jnp.int32, (64, B), 1) & 15
    for k in range(8):
        main = jnp.where((lane >> 3) == k % 2, lifted[:, 0:B], 0.0)
        tail = jnp.where((lane >> 1) == k, lifted[:, B:], 0.0)
        left[64 * k : 64 * k + 64, 0:B] = main.astype(BF16)
        left[64 * k : 64 * k + 64, B : 2 * B] = tail.astype(BF16)


def collect(place, got, tag_pick, spread, out):
    x = got[...]
    at, _, main, rank = message_columns(place)
    row = lax.broadcasted_iota(jnp.int32, (PART, NSPACE * MSG), 0).astype(F32)
    tags = jnp.dot(tag_pick[...], x, preferred_element_type=F32).astype(BF16)
    label = jnp.dot(tags, spread[...], preferred_element_type=F32)[0:1]
    goal = jnp.where(main, 8 * label + (24 + at - 8 * rank), 2 * label + (at - 18 - 2 * rank))
    goal = jnp.where(label > 0.5, goal, -1.0)
    route = jnp.where(row == goal, 1.0, 0.0).astype(BF16)
    part = jnp.dot(route, x, preferred_element_type=F32).astype(BF16)
    for j in range(NCHAN):
        out[j] = part


def heads(parts, features, left, fold, grad_out, share, grad, sem):
    def gather(at):
        return jnp.concatenate(
            [parts[PART * c + at : PART * c + at + 16] for c in range(NCHAN)], axis=0
        )

    tails = [gather(16 * k) for k in range(2)]
    mains = [gather(32 + 16 * k) for k in range(8)]
    lane = lax.broadcasted_iota(jnp.int32, (64, B), 1) & 15
    for pair in range(BLOCKS // 2):
        two = 128 * (pair % 4)
        right = jnp.concatenate([mains[pair], tails[pair // 4]], axis=0)
        both = jnp.dot(left[two : two + 128], right, preferred_element_type=F32).astype(BF16)
        for k in range(2):
            grad[:, (2 * pair + k) * B : (2 * pair + k + 1) * B] = both[64 * k : 64 * k + 64]
    copy = pltpu.make_async_copy(grad, grad_out, sem)
    copy.start()

    def block(b):
        return features[:, b * B : (b + 1) * B]

    def product(left, right):
        return lax.dot_general(left, right, (((1,), (1,)), ((), ())), preferred_element_type=F32)

    paired = [
        jnp.concatenate([block(2 * k + half) for k in range(8)], axis=1) for half in range(2)
    ]
    total_main = product(jnp.concatenate(paired, axis=0), jnp.concatenate(mains, axis=1))
    eight = [jnp.concatenate([block(k), block(8 + k)], axis=1) for k in range(8)]
    total_tail = product(jnp.concatenate(eight, axis=0), jnp.concatenate(tails, axis=1))
    main = jnp.where((lane >> 3) == 0, total_main[0:64], total_main[64:128])
    tail = total_tail[0:64]
    for k in range(1, 8):
        tail = jnp.where((lane >> 1) == k, total_tail[64 * k : 64 * k + 64], tail)
    total = jnp.dot(
        jnp.concatenate([main, tail], axis=1),
        fold[...],
        preferred_element_type=F32,
        precision=lax.Precision.HIGHEST,
    )
    full = lax.broadcasted_iota(jnp.int32, (64, B), 1)
    first = jnp.where(full < 64, total, 0.0)
    rest = jnp.where(full < 64, 0.0, total)
    front = first[0:32] + pltpu.roll(first[32:64], 64, 1)
    back = rest[32:40]
    for k in range(8):
        if k != 4:
            back = back + pltpu.roll(rest[8 * k : 8 * k + 8], (16 * k - 64) % B, 1)
    for j in range(GROUP):
        share[j, 0:32] = front
        share[j, 32:40] = back
    copy.wait()


def add_up(got):
    total = got[0]
    for j in range(1, GROUP):
        total = total + got[j]
    return total


def add_copies(got, out):
    total = add_up(got)
    for j in range(GROUP):
        out[j] = total


def add_last(scale, got, out):
    total = add_up(got) * scale
    front, back = total[0:32], total[32:40]
    out[0:32, 0:64] = front[:, 0:64]
    out[32:64, 0:64] = pltpu.roll(front, 64, 1)[:, 0:64]
    for k in range(8):
        out[8 * k : 8 * k + 8, 64:VARS] = pltpu.roll(back, (64 - 16 * k) % B, 1)[:, 64:VARS]


def tables():
    k = np.arange(256)
    c, i = (k % 128) // 16, k % 16
    var = OWN * c + np.where(k < 128, i % 8, 8 + i % 2)
    fold = var[:, None] == np.arange(B)[None]
    return fold.astype(np.float32)


def small_grant(mib):
    return pltpu.CompilerParams(vmem_limit_bytes=mib << 20)


def near(x):
    return pltpu.with_memory_space_constraint(x, pltpu.VMEM)


def far(x):
    return pltpu.with_memory_space_constraint(x, pltpu.HBM)


def on_device(cotangent, pair_band, pair_target, pair_count, pair_weight, head_weight, features):
    fold = tables()
    hp_local = features.shape[1]
    place = lax.axis_index(("chan",) + SPACE).astype(jnp.int32).reshape(1)
    hbm = pl.BlockSpec(memory_space=pltpu.HBM)
    sent, tag_pick, spread, left = pl.pallas_call(
        contribute,
        out_shape=(
            jax.ShapeDtypeStruct((NSPACE * MSG, B), BF16),
            jax.ShapeDtypeStruct((16, NSPACE * MSG), BF16),
            jax.ShapeDtypeStruct((SLOTS, NSPACE * MSG), BF16),
            jax.ShapeDtypeStruct((512, 2 * B), BF16),
        ),
        in_specs=[pl.BlockSpec(memory_space=pltpu.SMEM)] * 2 + [hbm] * 5,
        scratch_shapes=[
            pltpu.SMEM((SLOTS,), jnp.int32),
            pltpu.SMEM((SLOTS,), jnp.int32),
            pltpu.VMEM((VARS, BLOCKS * B), BF16),
            pltpu.VMEM(head_weight.shape, BF16),
            pltpu.VMEM((SLOTS, B, B), BF16),
            pltpu.VMEM((2 * BLOCKS + 1, 16, B), BF16),
            pltpu.VMEM((SLOTS, 16, B), F32),
            pltpu.SMEM((NSPACE,), jnp.int32),
            pltpu.SemaphoreType.DMA((SLOTS // CHUNK + 4,)),
        ],
        compiler_params=small_grant(12),
        name="contribute",
    )(
        place,
        pair_count,
        *map(far, (pair_band, pair_target, cotangent, head_weight, pair_weight)),
    )
    got = lax.all_to_all(sent.reshape(NSPACE, MSG // 2, 2, B), SPACE, 0, 0, tiled=True)
    parts = pl.pallas_call(
        collect,
        out_shape=jax.ShapeDtypeStruct((NCHAN, PART, B), BF16),
        in_specs=[pl.BlockSpec(memory_space=pltpu.SMEM)]
        + [pl.BlockSpec(memory_space=pltpu.VMEM)] * 3,
        compiler_params=small_grant(8),
        name="collect",
    )(place, near(got.reshape(NSPACE * MSG, B)), near(tag_pick), near(spread))
    parts = lax.all_to_all(parts, "chan", 0, 0, tiled=True).reshape(NCHAN * PART, B)
    parts = near(parts)
    feature_grad, share = pl.pallas_call(
        heads,
        out_shape=(
            jax.ShapeDtypeStruct((head_weight.shape[0], hp_local), BF16),
            jax.ShapeDtypeStruct((GROUP, 40, B), F32),
        ),
        out_specs=(hbm, pl.BlockSpec(memory_space=pltpu.VMEM)),
        scratch_shapes=[
            pltpu.VMEM((head_weight.shape[0], hp_local), BF16),
            pltpu.SemaphoreType.DMA(()),
        ],
        compiler_params=small_grant(8),
        name="heads",
    )(parts, features, near(left), fold)
    share = lax.all_to_all(share, ("x", "core"), 0, 0, tiled=True)
    share = pl.pallas_call(
        add_copies,
        out_shape=jax.ShapeDtypeStruct(share.shape, F32),
        compiler_params=small_grant(2),
        name="add_copies",
    )(near(share))
    share = lax.all_to_all(share, "y", 0, 0, tiled=True)
    grad_scale = float(hp_local * NSPACE) ** (-0.5)
    weight_grad = pl.pallas_call(
        functools.partial(add_last, grad_scale),
        out_shape=jax.ShapeDtypeStruct(head_weight.shape, F32),
        compiler_params=small_grant(2),
        name="add_last",
    )(near(share))
    return feature_grad, weight_grad


def solution(mesh):
    fine = Mesh(mesh.devices.reshape(NCHAN, 8, 4, 2), ("chan",) + SPACE)
    placed = (
        P(None, SPACE),
        P(SPACE),
        P(SPACE),
        P(SPACE),
        P(SPACE, None, None),
        P("chan", None),
        P("chan", SPACE),
    )
    return jax.shard_map(
        on_device,
        mesh=fine,
        in_specs=placed,
        out_specs=(P("chan", SPACE), P("chan", None)),
        check_vma=False,
    )
```

```python
import functools

import jax
import jax.numpy as jnp
import numpy as np
from jax import lax
from jax.experimental import pallas as pl
from jax.experimental.pallas import tpu as pltpu
from jax.sharding import Mesh
from jax.sharding import PartitionSpec as P

NCHAN = 8
NSPACE = 64
VARS = 80
B = 128
SLOTS = 128
BLOCKS = 16
OWN = VARS // NCHAN
MSG = 22
CHUNK = 32
PART = OWN * BLOCKS
GROUP = 8
SPACE = ("y", "x", "core")
F32 = jnp.float32
BF16 = jnp.bfloat16


def contribute(
    place, count, band_in, target_in, cot_in, head_in, weight_in, out, tag_pick, spread, left,
    band, target, cot, head, weight, lhs, acc, seen, sems,
):
    chunks = SLOTS // CHUNK
    small = [
        pltpu.make_async_copy(src, dst, sems.at[chunks + k])
        for k, (src, dst) in enumerate(
            ((cot_in, cot), (band_in, band), (target_in, target), (head_in, head))
        )
    ]

    def part(k):
        at = pl.ds(pl.multiple_of(k * CHUNK, CHUNK), CHUNK)
        return pltpu.make_async_copy(weight_in.at[at], weight.at[at], sems.at[k])

    for copy in small:
        copy.start()
    live_slots = count[0]
    groups = (live_slots + (CHUNK - 1)) // CHUNK
    for k in range(chunks):

        @pl.when(k < groups)
        def _():
            part(k).start()

    mine = place[0] // NSPACE
    space = place[0] % NSPACE
    for j in range(NSPACE):
        seen[j] = 2 * j
    row = lax.broadcasted_iota(jnp.int32, (32, VARS), 0)
    col = lax.broadcasted_iota(jnp.int32, (32, VARS), 1)
    low = row & 15
    tail = low - 8 - 2 * (row >> 4)
    var = jnp.where(low < 8, low, jnp.where((tail >= 0) & (tail < 2), 8 + tail, -VARS * NCHAN))
    pick = jnp.where(col == var + mine * OWN, 1.0, 0.0).astype(BF16)
    tag_row = lax.broadcasted_iota(jnp.int32, (8, B), 0)
    tag_lane = lax.broadcasted_iota(jnp.int32, (8, B), 1)
    tag_lane = jnp.where(tag_row == 4, tag_lane - 2 * space, -1)
    dead = 2 * BLOCKS
    lhs[dead] = jnp.zeros((16, B), BF16)
    acc[...] = jnp.zeros_like(acc)
    at, src, _, rank = message_columns(place)
    lane = lax.broadcasted_iota(jnp.int32, (SLOTS, NSPACE * MSG), 0).astype(F32)
    slot_of = jnp.where(at < 19.5, 2 * src + rank, -1.0)
    spread[...] = jnp.where(lane == slot_of, 1.0, 0.0).astype(BF16)
    tag_row_of = jnp.where(jnp.abs(at - 20) < 0.5, 0.0, -1.0)
    tag_pick[...] = jnp.where(lane[0:16] == tag_row_of, 1.0, 0.0).astype(BF16)
    small[3].wait()
    left_operands(head, left)
    small[0].wait()
    rows = jnp.dot(pick, cot[...], preferred_element_type=F32).astype(BF16)
    for j in range(BLOCKS):
        for rank in range(2):
            lhs[2 * j + rank] = rows[16 * rank : 16 * rank + 16, j * B : (j + 1) * B]
    for copy in small[1:3]:
        copy.wait()

    def chunk(k, carry):
        part(k).wait()
        for i in range(CHUNK):
            slot = k * CHUNK + i
            goal = target[slot]
            dest = goal >> 4
            key = seen[dest]
            seen[dest] = key + 1
            rank = key & 1
            live = slot < live_slots
            source = jnp.where(live, 2 * band[slot] + rank, dead)
            tag = jnp.where(live, (goal & 15) + 1, 0)
            value = jnp.dot(lhs[source], weight[slot], preferred_element_type=F32)
            acc[key, 0:8, :] = value[0:8]
            acc[key, 8:16, :] = value[8:16] + jnp.where(tag_lane == rank, tag, 0).astype(F32)
        return carry

    lax.fori_loop(0, groups, chunk, 0)

    sub = lax.broadcasted_iota(jnp.int32, (8, B), 0)

    def emit(k, carry):
        tiles = []
        for quad in range(2):
            first, second, extra, turned = [], [], [], []
            for h in range(4):
                one, two = acc[16 * k + 8 * quad + 2 * h], acc[16 * k + 8 * quad + 2 * h + 1]
                first.append(one[0:8])
                second.append(two[0:8])
                extra.append(one[8:16] + two[8:16])
                turned.append(pltpu.roll(extra[h], 2, 0))
            for h in range(4):
                tiles += [first[h], second[h]]
                if h < 3:
                    tiles.append(jnp.where(sub < 6 - 2 * h, extra[h], turned[h + 1]))
        rows = jnp.concatenate(tiles, axis=0).astype(BF16)
        out[pl.ds(pl.multiple_of(8 * MSG * k, 8 * MSG), 8 * MSG), :] = rows
        return carry

    lax.fori_loop(0, NSPACE // 8, emit, 0, unroll=4)


def message_columns(place):
    j = lax.broadcasted_iota(jnp.int32, (1, NSPACE * MSG), 1).astype(F32)
    src = jnp.floor((j + 0.5) * (1.0 / MSG))
    at = j - MSG * src - (2 * (place[0] & 3)).astype(F32)
    at = jnp.where(at < 0, at + MSG, at)
    main = at < 15.5
    rank = jnp.where(main, jnp.where(at < 7.5, 0.0, 1.0), jnp.where(at < 17.5, 0.0, 1.0))
    return at, src, main, rank


def left_operands(head, left):
    var = lax.broadcasted_iota(jnp.int32, (VARS, 2 * B), 0)
    col = lax.broadcasted_iota(jnp.int32, (VARS, 2 * B), 1)
    own = jnp.where(col < B, col & 7, 8 + (col & 1))
    proj = jnp.where(var == OWN * ((col & (B - 1)) >> 4) + own, 1.0, 0.0).astype(BF16)
    lifted = jnp.dot(head[...], proj, preferred_element_type=F32)
    lane = lax.broadcasted_iota(jnp.int32, (64, B), 1) & 15
    for k in range(8):
        main = jnp.where((lane >> 3) == k % 2, lifted[:, 0:B], 0.0)
        tail = jnp.where((lane >> 1) == k, lifted[:, B:], 0.0)
        left[64 * k : 64 * k + 64, 0:B] = main.astype(BF16)
        left[64 * k : 64 * k + 64, B : 2 * B] = tail.astype(BF16)


def collect(place, got, tag_pick, spread, out):
    x = got[...]
    at, _, main, rank = message_columns(place)
    row = lax.broadcasted_iota(jnp.int32, (PART, NSPACE * MSG), 0).astype(F32)
    tags = jnp.dot(tag_pick[...], x, preferred_element_type=F32).astype(BF16)
    label = jnp.dot(tags, spread[...], preferred_element_type=F32)[0:1]
    goal = jnp.where(main, 8 * label + (24 + at - 8 * rank), 2 * label + (at - 18 - 2 * rank))
    goal = jnp.where(label > 0.5, goal, -1.0)
    route = jnp.where(row == goal, 1.0, 0.0).astype(BF16)
    part = jnp.dot(route, x, preferred_element_type=F32).astype(BF16)
    for j in range(NCHAN):
        out[j] = part


def heads(parts, features, left, fold, grad_out, share, grad, sem):
    def gather(at):
        return jnp.concatenate(
            [parts[PART * c + at : PART * c + at + 16] for c in range(NCHAN)], axis=0
        )

    tails = [gather(16 * k) for k in range(2)]
    mains = [gather(32 + 16 * k) for k in range(8)]
    lane = lax.broadcasted_iota(jnp.int32, (64, B), 1) & 15
    for half in range(2):
        below = jnp.dot(left[:, B:], tails[half], preferred_element_type=F32)
        for k in range(4):
            pair = 4 * half + k
            both = jnp.dot(left[0 : 2 * 64, 0:B], mains[pair], preferred_element_type=F32)
            both = (both + below[128 * k : 128 * k + 128]).astype(BF16)
            for one in range(2):
                at = (2 * pair + one) * B
                grad[:, at : at + B] = both[64 * one : 64 * one + 64]
    copy = pltpu.make_async_copy(grad, grad_out, sem)
    copy.start()

    def block(b):
        return features[:, b * B : (b + 1) * B]

    def product(left, right):
        return lax.dot_general(left, right, (((1,), (1,)), ((), ())), preferred_element_type=F32)

    paired = [
        jnp.concatenate([block(2 * k + half) for k in range(8)], axis=1) for half in range(2)
    ]
    total_main = product(jnp.concatenate(paired, axis=0), jnp.concatenate(mains, axis=1))
    eight = [jnp.concatenate([block(k), block(8 + k)], axis=1) for k in range(8)]
    total_tail = product(jnp.concatenate(eight, axis=0), jnp.concatenate(tails, axis=1))
    main = jnp.where((lane >> 3) == 0, total_main[0:64], total_main[64:128])
    tail = total_tail[0:64]
    for k in range(1, 8):
        tail = jnp.where((lane >> 1) == k, total_tail[64 * k : 64 * k + 64], tail)
    total = jnp.dot(
        jnp.concatenate([main, tail], axis=1),
        fold[...],
        preferred_element_type=F32,
        precision=lax.Precision.HIGHEST,
    )
    full = lax.broadcasted_iota(jnp.int32, (64, B), 1)
    first = jnp.where(full < 64, total, 0.0)
    rest = jnp.where(full < 64, 0.0, total)
    front = first[0:32] + pltpu.roll(first[32:64], 64, 1)
    back = rest[32:40]
    for k in range(8):
        if k != 4:
            back = back + pltpu.roll(rest[8 * k : 8 * k + 8], (16 * k - 64) % B, 1)
    for j in range(GROUP):
        share[j, 0:32] = front
        share[j, 32:40] = back
    copy.wait()


def add_up(got):
    total = got[0]
    for j in range(1, GROUP):
        total = total + got[j]
    return total


def add_copies(got, out):
    total = add_up(got)
    for j in range(GROUP):
        out[j] = total


def add_last(scale, got, out):
    total = add_up(got) * scale
    front, back = total[0:32], total[32:40]
    out[0:32, 0:64] = front[:, 0:64]
    out[32:64, 0:64] = pltpu.roll(front, 64, 1)[:, 0:64]
    for k in range(8):
        out[8 * k : 8 * k + 8, 64:VARS] = pltpu.roll(back, (64 - 16 * k) % B, 1)[:, 64:VARS]


def tables():
    k = np.arange(256)
    c, i = (k % 128) // 16, k % 16
    var = OWN * c + np.where(k < 128, i % 8, 8 + i % 2)
    fold = var[:, None] == np.arange(B)[None]
    return fold.astype(np.float32)


def small_grant(mib):
    return pltpu.CompilerParams(vmem_limit_bytes=mib << 20)


def near(x):
    return pltpu.with_memory_space_constraint(x, pltpu.VMEM)


def far(x):
    return pltpu.with_memory_space_constraint(x, pltpu.HBM)


def on_device(cotangent, pair_band, pair_target, pair_count, pair_weight, head_weight, features):
    fold = tables()
    hp_local = features.shape[1]
    place = lax.axis_index(("chan",) + SPACE).astype(jnp.int32).reshape(1)
    hbm = pl.BlockSpec(memory_space=pltpu.HBM)
    sent, tag_pick, spread, left = pl.pallas_call(
        contribute,
        out_shape=(
            jax.ShapeDtypeStruct((NSPACE * MSG, B), BF16),
            jax.ShapeDtypeStruct((16, NSPACE * MSG), BF16),
            jax.ShapeDtypeStruct((SLOTS, NSPACE * MSG), BF16),
            jax.ShapeDtypeStruct((512, 2 * B), BF16),
        ),
        in_specs=[pl.BlockSpec(memory_space=pltpu.SMEM)] * 2 + [hbm] * 5,
        scratch_shapes=[
            pltpu.SMEM((SLOTS,), jnp.int32),
            pltpu.SMEM((SLOTS,), jnp.int32),
            pltpu.VMEM((VARS, BLOCKS * B), BF16),
            pltpu.VMEM(head_weight.shape, BF16),
            pltpu.VMEM((SLOTS, B, B), BF16),
            pltpu.VMEM((2 * BLOCKS + 1, 16, B), BF16),
            pltpu.VMEM((SLOTS, 16, B), F32),
            pltpu.SMEM((NSPACE,), jnp.int32),
            pltpu.SemaphoreType.DMA((SLOTS // CHUNK + 4,)),
        ],
        compiler_params=small_grant(12),
        name="contribute",
    )(
        place,
        pair_count,
        *map(far, (pair_band, pair_target, cotangent, head_weight, pair_weight)),
    )
    got = lax.all_to_all(sent.reshape(NSPACE, MSG // 2, 2, B), SPACE, 0, 0, tiled=True)
    parts = pl.pallas_call(
        collect,
        out_shape=jax.ShapeDtypeStruct((NCHAN, PART, B), BF16),
        in_specs=[pl.BlockSpec(memory_space=pltpu.SMEM)]
        + [pl.BlockSpec(memory_space=pltpu.VMEM)] * 3,
        compiler_params=small_grant(8),
        name="collect",
    )(place, near(got.reshape(NSPACE * MSG, B)), near(tag_pick), near(spread))
    parts = lax.all_to_all(parts, "chan", 0, 0, tiled=True).reshape(NCHAN * PART, B)
    parts = near(parts)
    feature_grad, share = pl.pallas_call(
        heads,
        out_shape=(
            jax.ShapeDtypeStruct((head_weight.shape[0], hp_local), BF16),
            jax.ShapeDtypeStruct((GROUP, 40, B), F32),
        ),
        out_specs=(hbm, pl.BlockSpec(memory_space=pltpu.VMEM)),
        scratch_shapes=[
            pltpu.VMEM((head_weight.shape[0], hp_local), BF16),
            pltpu.SemaphoreType.DMA(()),
        ],
        compiler_params=small_grant(8),
        name="heads",
    )(parts, features, near(left), fold)
    share = lax.all_to_all(share, ("x", "core"), 0, 0, tiled=True)
    share = pl.pallas_call(
        add_copies,
        out_shape=jax.ShapeDtypeStruct(share.shape, F32),
        compiler_params=small_grant(2),
        name="add_copies",
    )(near(share))
    share = lax.all_to_all(share, "y", 0, 0, tiled=True)
    grad_scale = float(hp_local * NSPACE) ** (-0.5)
    weight_grad = pl.pallas_call(
        functools.partial(add_last, grad_scale),
        out_shape=jax.ShapeDtypeStruct(head_weight.shape, F32),
        compiler_params=small_grant(2),
        name="add_last",
    )(near(share))
    return feature_grad, weight_grad


def solution(mesh):
    fine = Mesh(mesh.devices.reshape(NCHAN, 8, 4, 2), ("chan",) + SPACE)
    placed = (
        P(None, SPACE),
        P(SPACE),
        P(SPACE),
        P(SPACE),
        P(SPACE, None, None),
        P("chan", None),
        P("chan", SPACE),
    )
    return jax.shard_map(
        on_device,
        mesh=fine,
        in_specs=placed,
        out_specs=(P("chan", SPACE), P("chan", None)),
        check_vma=False,
    )
```

```python
import functools

import jax
import jax.numpy as jnp
import numpy as np
from jax import lax
from jax.experimental import pallas as pl
from jax.experimental.pallas import tpu as pltpu
from jax.sharding import Mesh
from jax.sharding import PartitionSpec as P

NCHAN = 8
NSPACE = 64
VARS = 80
B = 128
SLOTS = 128
BLOCKS = 16
OWN = VARS // NCHAN
MSG = 22
CHUNK = 32
PART = OWN * BLOCKS
GROUP = 8
SPACE = ("y", "x", "core")
F32 = jnp.float32
BF16 = jnp.bfloat16


def contribute(
    place, count, band_in, target_in, cot_in, head_in, weight_in, out, tag_pick, spread, left,
    band, target, cot, head, weight, lhs, acc, seen, sems,
):
    chunks = SLOTS // CHUNK
    small = [
        pltpu.make_async_copy(src, dst, sems.at[chunks + k])
        for k, (src, dst) in enumerate(
            ((cot_in, cot), (band_in, band), (target_in, target), (head_in, head))
        )
    ]

    def part(k):
        at = pl.ds(pl.multiple_of(k * CHUNK, CHUNK), CHUNK)
        return pltpu.make_async_copy(weight_in.at[at], weight.at[at], sems.at[k])

    for copy in small:
        copy.start()
    live_slots = count[0]
    groups = (live_slots + (CHUNK - 1)) // CHUNK
    for k in range(chunks):

        @pl.when(k < groups)
        def _():
            part(k).start()

    mine = place[0] // NSPACE
    space = place[0] % NSPACE
    for j in range(NSPACE):
        seen[j] = 2 * j
    row = lax.broadcasted_iota(jnp.int32, (32, VARS), 0)
    col = lax.broadcasted_iota(jnp.int32, (32, VARS), 1)
    low = row & 15
    tail = low - 8 - 2 * (row >> 4)
    var = jnp.where(low < 8, low, jnp.where((tail >= 0) & (tail < 2), 8 + tail, -VARS * NCHAN))
    pick = jnp.where(col == var + mine * OWN, 1.0, 0.0).astype(BF16)
    tag_row = lax.broadcasted_iota(jnp.int32, (8, B), 0)
    tag_lane = lax.broadcasted_iota(jnp.int32, (8, B), 1)
    tag_lane = jnp.where(tag_row == 4, tag_lane - 2 * space, -1)
    dead = 2 * BLOCKS
    lhs[dead] = jnp.zeros((16, B), BF16)
    acc[...] = jnp.zeros_like(acc)
    at, src, _, rank = message_columns(place)
    lane = lax.broadcasted_iota(jnp.int32, (SLOTS, NSPACE * MSG), 0).astype(F32)
    slot_of = jnp.where(at < 19.5, 2 * src + rank, -1.0)
    spread[...] = jnp.where(lane == slot_of, 1.0, 0.0).astype(BF16)
    tag_row_of = jnp.where(jnp.abs(at - 20) < 0.5, 0.0, -1.0)
    tag_pick[...] = jnp.where(lane[0:16] == tag_row_of, 1.0, 0.0).astype(BF16)
    small[3].wait()
    left_operands(head, left)
    small[0].wait()
    rows = jnp.dot(pick, cot[...], preferred_element_type=F32).astype(BF16)
    for j in range(BLOCKS):
        for rank in range(2):
            lhs[2 * j + rank] = rows[16 * rank : 16 * rank + 16, j * B : (j + 1) * B]
    for copy in small[1:3]:
        copy.wait()

    def chunk(k, carry):
        part(k).wait()
        for i in range(CHUNK):
            slot = k * CHUNK + i
            goal = target[slot]
            dest = goal >> 4
            key = seen[dest]
            seen[dest] = key + 1
            rank = key & 1
            live = slot < live_slots
            source = jnp.where(live, 2 * band[slot] + rank, dead)
            tag = jnp.where(live, (goal & 15) + 1, 0)
            value = jnp.dot(lhs[source], weight[slot], preferred_element_type=F32)
            acc[key, 0:8, :] = value[0:8]
            acc[key, 8:16, :] = value[8:16] + jnp.where(tag_lane == rank, tag, 0).astype(F32)
        return carry

    lax.fori_loop(0, groups, chunk, 0)

    sub = lax.broadcasted_iota(jnp.int32, (8, B), 0)

    def emit(k, carry):
        tiles = []
        for quad in range(2):
            first, second, extra, turned = [], [], [], []
            for h in range(4):
                one, two = acc[16 * k + 8 * quad + 2 * h], acc[16 * k + 8 * quad + 2 * h + 1]
                first.append(one[0:8])
                second.append(two[0:8])
                extra.append(one[8:16] + two[8:16])
                turned.append(pltpu.roll(extra[h], 2, 0))
            for h in range(4):
                tiles += [first[h], second[h]]
                if h < 3:
                    tiles.append(jnp.where(sub < 6 - 2 * h, extra[h], turned[h + 1]))
        rows = jnp.concatenate(tiles, axis=0).astype(BF16)
        out[pl.ds(pl.multiple_of(8 * MSG * k, 8 * MSG), 8 * MSG), :] = rows
        return carry

    lax.fori_loop(0, NSPACE // 8, emit, 0, unroll=4)


def message_columns(place):
    j = lax.broadcasted_iota(jnp.int32, (1, NSPACE * MSG), 1).astype(F32)
    src = jnp.floor((j + 0.5) * (1.0 / MSG))
    at = j - MSG * src - (2 * (place[0] & 3)).astype(F32)
    at = jnp.where(at < 0, at + MSG, at)
    main = at < 15.5
    rank = jnp.where(main, jnp.where(at < 7.5, 0.0, 1.0), jnp.where(at < 17.5, 0.0, 1.0))
    return at, src, main, rank


def left_operands(head, left):
    var = lax.broadcasted_iota(jnp.int32, (VARS, 2 * B), 0)
    col = lax.broadcasted_iota(jnp.int32, (VARS, 2 * B), 1)
    own = jnp.where(col < B, col & 7, 8 + (col & 1))
    proj = jnp.where(var == OWN * ((col & (B - 1)) >> 4) + own, 1.0, 0.0).astype(BF16)
    lifted = jnp.dot(head[...], proj, preferred_element_type=F32)
    lane = lax.broadcasted_iota(jnp.int32, (64, B), 1) & 15
    for k in range(8):
        main = jnp.where((lane >> 3) == k % 2, lifted[:, 0:B], 0.0)
        tail = jnp.where((lane >> 1) == k, lifted[:, B:], 0.0)
        left[64 * k : 64 * k + 64, 0:B] = main.astype(BF16)
        left[64 * k : 64 * k + 64, B : 2 * B] = tail.astype(BF16)


def collect(place, got, tag_pick, spread, out):
    x = got[...]
    at, _, main, rank = message_columns(place)
    row = lax.broadcasted_iota(jnp.int32, (PART, B), 0).astype(F32).astype(BF16)
    row = jnp.concatenate([row] * (NSPACE * MSG // B), axis=1)
    tags = jnp.dot(tag_pick[...], x, preferred_element_type=F32).astype(BF16)
    label = jnp.dot(tags, spread[...], preferred_element_type=F32)[0:1]
    goal = jnp.where(main, 8 * label + (24 + at - 8 * rank), 2 * label + (at - 18 - 2 * rank))
    goal = jnp.where(label > 0.5, goal, -1.0)
    route = jnp.where(row == goal.astype(BF16), jnp.ones((), BF16), jnp.zeros((), BF16))
    part = jnp.dot(route, x, preferred_element_type=F32).astype(BF16)
    for j in range(NCHAN):
        out[j] = part


def heads(parts, features, left, fold, grad_out, share, grad, sem):
    def gather(at):
        return jnp.concatenate(
            [parts[PART * c + at : PART * c + at + 16] for c in range(NCHAN)], axis=0
        )

    tails = [gather(16 * k) for k in range(2)]
    mains = [gather(32 + 16 * k) for k in range(8)]
    lane = lax.broadcasted_iota(jnp.int32, (64, B), 1) & 15
    for half in range(2):
        below = jnp.dot(left[:, B:], tails[half], preferred_element_type=F32)
        for k in range(4):
            pair = 4 * half + k
            both = jnp.dot(left[0 : 2 * 64, 0:B], mains[pair], preferred_element_type=F32)
            both = (both + below[128 * k : 128 * k + 128]).astype(BF16)
            for one in range(2):
                at = (2 * pair + one) * B
                grad[:, at : at + B] = both[64 * one : 64 * one + 64]
    copy = pltpu.make_async_copy(grad, grad_out, sem)
    copy.start()

    def block(b):
        return features[:, b * B : (b + 1) * B]

    def product(left, right):
        return lax.dot_general(left, right, (((1,), (1,)), ((), ())), preferred_element_type=F32)

    paired = [
        jnp.concatenate([block(2 * k + half) for k in range(8)], axis=1) for half in range(2)
    ]
    total_main = product(jnp.concatenate(paired, axis=0), jnp.concatenate(mains, axis=1))
    eight = [jnp.concatenate([block(k), block(8 + k)], axis=1) for k in range(8)]
    total_tail = product(jnp.concatenate(eight, axis=0), jnp.concatenate(tails, axis=1))
    main = jnp.where((lane >> 3) == 0, total_main[0:64], total_main[64:128])
    tail = total_tail[0:64]
    for k in range(1, 8):
        tail = jnp.where((lane >> 1) == k, total_tail[64 * k : 64 * k + 64], tail)
    total = jnp.dot(
        jnp.concatenate([main, tail], axis=1),
        fold[...],
        preferred_element_type=F32,
        precision=lax.Precision.HIGHEST,
    )
    full = lax.broadcasted_iota(jnp.int32, (64, B), 1)
    first = jnp.where(full < 64, total, 0.0)
    rest = jnp.where(full < 64, 0.0, total)
    front = first[0:32] + pltpu.roll(first[32:64], 64, 1)
    back = rest[32:40]
    for k in range(8):
        if k != 4:
            back = back + pltpu.roll(rest[8 * k : 8 * k + 8], (16 * k - 64) % B, 1)
    for j in range(GROUP):
        share[j, 0:32] = front
        share[j, 32:40] = back
    copy.wait()


def add_up(got):
    total = got[0]
    for j in range(1, GROUP):
        total = total + got[j]
    return total


def add_copies(got, out):
    total = add_up(got)
    for j in range(GROUP):
        out[j] = total


def add_last(scale, got, out):
    total = add_up(got) * scale
    front, back = total[0:32], total[32:40]
    out[0:32, 0:64] = front[:, 0:64]
    out[32:64, 0:64] = pltpu.roll(front, 64, 1)[:, 0:64]
    for k in range(8):
        out[8 * k : 8 * k + 8, 64:VARS] = pltpu.roll(back, (64 - 16 * k) % B, 1)[:, 64:VARS]


def tables():
    k = np.arange(256)
    c, i = (k % 128) // 16, k % 16
    var = OWN * c + np.where(k < 128, i % 8, 8 + i % 2)
    fold = var[:, None] == np.arange(B)[None]
    return fold.astype(np.float32)


def small_grant(mib):
    return pltpu.CompilerParams(vmem_limit_bytes=mib << 20)


def near(x):
    return pltpu.with_memory_space_constraint(x, pltpu.VMEM)


def far(x):
    return pltpu.with_memory_space_constraint(x, pltpu.HBM)


def on_device(cotangent, pair_band, pair_target, pair_count, pair_weight, head_weight, features):
    fold = tables()
    hp_local = features.shape[1]
    place = lax.axis_index(("chan",) + SPACE).astype(jnp.int32).reshape(1)
    hbm = pl.BlockSpec(memory_space=pltpu.HBM)
    sent, tag_pick, spread, left = pl.pallas_call(
        contribute,
        out_shape=(
            jax.ShapeDtypeStruct((NSPACE * MSG, B), BF16),
            jax.ShapeDtypeStruct((16, NSPACE * MSG), BF16),
            jax.ShapeDtypeStruct((SLOTS, NSPACE * MSG), BF16),
            jax.ShapeDtypeStruct((512, 2 * B), BF16),
        ),
        in_specs=[pl.BlockSpec(memory_space=pltpu.SMEM)] * 2 + [hbm] * 5,
        scratch_shapes=[
            pltpu.SMEM((SLOTS,), jnp.int32),
            pltpu.SMEM((SLOTS,), jnp.int32),
            pltpu.VMEM((VARS, BLOCKS * B), BF16),
            pltpu.VMEM(head_weight.shape, BF16),
            pltpu.VMEM((SLOTS, B, B), BF16),
            pltpu.VMEM((2 * BLOCKS + 1, 16, B), BF16),
            pltpu.VMEM((SLOTS, 16, B), F32),
            pltpu.SMEM((NSPACE,), jnp.int32),
            pltpu.SemaphoreType.DMA((SLOTS // CHUNK + 4,)),
        ],
        compiler_params=small_grant(12),
        name="contribute",
    )(
        place,
        pair_count,
        *map(far, (pair_band, pair_target, cotangent, head_weight, pair_weight)),
    )
    got = lax.all_to_all(sent.reshape(NSPACE, MSG // 2, 2, B), SPACE, 0, 0, tiled=True)
    parts = pl.pallas_call(
        collect,
        out_shape=jax.ShapeDtypeStruct((NCHAN, PART, B), BF16),
        in_specs=[pl.BlockSpec(memory_space=pltpu.SMEM)]
        + [pl.BlockSpec(memory_space=pltpu.VMEM)] * 3,
        compiler_params=small_grant(8),
        name="collect",
    )(place, near(got.reshape(NSPACE * MSG, B)), near(tag_pick), near(spread))
    parts = lax.all_to_all(parts, "chan", 0, 0, tiled=True).reshape(NCHAN * PART, B)
    parts = near(parts)
    feature_grad, share = pl.pallas_call(
        heads,
        out_shape=(
            jax.ShapeDtypeStruct((head_weight.shape[0], hp_local), BF16),
            jax.ShapeDtypeStruct((GROUP, 40, B), F32),
        ),
        out_specs=(hbm, pl.BlockSpec(memory_space=pltpu.VMEM)),
        scratch_shapes=[
            pltpu.VMEM((head_weight.shape[0], hp_local), BF16),
            pltpu.SemaphoreType.DMA(()),
        ],
        compiler_params=small_grant(8),
        name="heads",
    )(parts, features, near(left), fold)
    share = lax.all_to_all(share, ("x", "core"), 0, 0, tiled=True)
    share = pl.pallas_call(
        add_copies,
        out_shape=jax.ShapeDtypeStruct(share.shape, F32),
        compiler_params=small_grant(2),
        name="add_copies",
    )(near(share))
    share = lax.all_to_all(share, "y", 0, 0, tiled=True)
    grad_scale = float(hp_local * NSPACE) ** (-0.5)
    weight_grad = pl.pallas_call(
        functools.partial(add_last, grad_scale),
        out_shape=jax.ShapeDtypeStruct(head_weight.shape, F32),
        compiler_params=small_grant(2),
        name="add_last",
    )(near(share))
    return feature_grad, weight_grad


def solution(mesh):
    fine = Mesh(mesh.devices.reshape(NCHAN, 8, 4, 2), ("chan",) + SPACE)
    placed = (
        P(None, SPACE),
        P(SPACE),
        P(SPACE),
        P(SPACE),
        P(SPACE, None, None),
        P("chan", None),
        P("chan", SPACE),
    )
    return jax.shard_map(
        on_device,
        mesh=fine,
        in_specs=placed,
        out_specs=(P("chan", SPACE), P("chan", None)),
        check_vma=False,
    )
```
